256 devices in a mesh: row: 16 (over y_hi, z), col: 16 (over x, y_lo, core).
Axes of the slice: x: 4, y: 4 (y_hi: 2, y_lo: 2; y = y_hi * 2 + y_lo), z: 8, core: 2. Of those that a mesh axis runs over, the one named last changes fastest.
Arguments:
- pair_map: bfloat16 [64, 8192, 128], P('row', 'col'), may hold values from -6 to 6
- norm_gain: float32 [128], replicated, may hold values from 0.5 to 1.5
- in_weights: bfloat16 [3, 128, 512], replicated, may hold values from -0.5 to 0.5
- head_gain: float32 [3, 128], replicated, may hold values from 0.5 to 1.5
- out_weights: bfloat16 [3, 128, 128], replicated, may hold values from -0.5 to 0.5
- trans_gain: float32 [128], replicated, may hold values from 0.5 to 1.5
- up_weight: bfloat16 [128, 512], replicated, may hold values from -0.5 to 0.5
- down_weight: bfloat16 [512, 128], replicated, may hold values from -0.25 to 0.25
Outputs:
- result: bfloat16 [64, 8192, 128], P('row', 'col')
The draws below stay inside these ranges and needn't reach their ends.
All inputs are finite; a program needn't handle non-finite values.
Results may differ from the reference program's by a relative error of at most 0.012.
Values may be sent and summed in bfloat16 or wider, within the bound.
A program may use at most 64 MiB of HBM per device.

```python
import jax
import jax.numpy as jnp
from jax import lax

D = 128
HEADS = 4
HEAD = 32
FF = 512
ROW_DEV = 4
ROWS = 64
COLS = 8192
N_ROW = 16


def block_levels(key, extent, split, low, high):
    loudness = 1.0
    for axis_at, parts in split:
        heights = jax.random.uniform(jax.random.fold_in(jax.random.fold_in(key, 6), axis_at), (parts,), jnp.float32, low / len(split), high / len(split))
        loudness = loudness * jnp.repeat(jnp.exp(heights), extent[axis_at] // parts).reshape((-1,) + (1,) * (len(extent) - 1 - axis_at))
    return loudness


def noise(stream_key, shape, scale, limit, cuts=(), dtype=jnp.bfloat16):
    values = jax.random.normal(stream_key, shape, jnp.float32) * scale
    if len(cuts) > 0:
        values = block_levels(stream_key, shape, cuts, -0.22, 0.18) * values
    return jnp.clip(values, min=-limit, max=limit).astype(dtype)


def setup_inputs(seed: int = 0) -> dict:
    arg_keys = jax.random.split(jax.random.key(seed), 9)
    pair_map = noise(arg_keys[0], (ROWS, COLS, D), 1.0, 6.0, ((0, 16), (1, 16)))
    norm_gain = jnp.clip(1.0 + 0.1 * jax.random.normal(arg_keys[1], (D,), jnp.float32), 0.5, 1.5)
    in_weights = noise(arg_keys[2], (3, D, 4 * D), D ** -0.5, 0.5)
    head_gain = jnp.clip(1.0 + 0.1 * jax.random.normal(arg_keys[3], (3, D), jnp.float32), 0.5, 1.5)
    out_weights = noise(arg_keys[4], (3, D, D), D ** -0.5, 0.5)
    trans_gain = jnp.clip(1.0 + 0.1 * jax.random.normal(arg_keys[5], (D,), jnp.float32), 0.5, 1.5)
    up_weight = noise(arg_keys[6], (D, FF), D ** -0.5, 0.5)
    down_weight = noise(arg_keys[7], (FF, D), FF ** -0.5, 0.25)
    return dict(pair_map=pair_map, norm_gain=norm_gain, in_weights=in_weights, head_gain=head_gain, out_weights=out_weights, trans_gain=trans_gain, up_weight=up_weight, down_weight=down_weight)


epsilon = 1e-05

def feature(values):
    return jnp.where(values > 0, values + 1.0, jnp.exp(jnp.minimum(values, 0.0)))

def normalize(values, gain):
    meansq = lax.optimization_barrier(jnp.mean(values * values, axis=-1, keepdims=True))
    return values * lax.rsqrt(meansq + epsilon) * gain

def open_branch(normed, weight):
    width = weight.shape[0]
    flat = jnp.dot(normed.reshape(-1, width), weight, preferred_element_type=jnp.float32)
    shape = normed.shape[:-1] + (HEADS, HEAD)
    query_feat = feature(flat[:, :width]).astype(jnp.bfloat16).reshape(shape)
    key_feat = feature(flat[:, width:2 * width]).astype(jnp.bfloat16).reshape(shape)
    value_rows = flat[:, 2 * width:3 * width].astype(jnp.bfloat16).reshape(shape)
    gate_vals = jax.nn.sigmoid(flat[:, 3 * width:]).reshape(normed.shape)
    return (query_feat, key_feat, value_rows, gate_vals)

def close_branch(head_out, gate_vals, gain, weight):
    mixed_out = (normalize(head_out.reshape(gate_vals.shape), gain) * gate_vals).astype(jnp.bfloat16)
    width = weight.shape[0]
    projected = jnp.dot(mixed_out.reshape(-1, width), weight, preferred_element_type=jnp.float32)
    return projected.reshape(gate_vals.shape).astype(jnp.bfloat16)

def reference(pair_map, norm_gain, in_weights, head_gain, out_weights, trans_gain, up_weight, down_weight):
    blocks = pair_map.reshape(N_ROW, ROW_DEV, COLS, D)

    def first_pass(column_acc, block):
        normed = normalize(block.astype(jnp.float32), norm_gain).astype(jnp.bfloat16)
        outputs = []
        for branch in range(2):
            query_feat, key_feat, value_rows, gate_vals = open_branch(normed, in_weights[branch])
            states = jnp.einsum('rcha,rchb->rhab', key_feat.astype(jnp.float32), value_rows.astype(jnp.float32)).astype(jnp.bfloat16)
            head_out = jnp.einsum('rcha,rhab->rchb', query_feat.astype(jnp.float32), states.astype(jnp.float32))
            outputs.append(close_branch(head_out, gate_vals, head_gain[branch], out_weights[branch]))
        query_feat, key_feat, value_rows, gate_vals = open_branch(normed, in_weights[2])
        column_acc = column_acc + jnp.einsum('rcha,rchb->chab', key_feat.astype(jnp.float32), value_rows.astype(jnp.float32))
        return (column_acc, (outputs[0], outputs[1]))
    column_zero = jnp.zeros((COLS, HEADS, HEAD, HEAD), jnp.float32)
    column_acc, (first_out, second_out) = lax.scan(first_pass, column_zero, blocks)
    column_states = column_acc.astype(jnp.bfloat16).astype(jnp.float32)

    def second_pass(inputs):
        block, first_rows, second_rows = inputs
        widened = block.astype(jnp.float32)
        normed = normalize(widened, norm_gain).astype(jnp.bfloat16)
        query_feat, key_feat, value_rows, gate_vals = open_branch(normed, in_weights[2])
        head_out = jnp.einsum('rcha,chab->rchb', query_feat.astype(jnp.float32), column_states)
        third_rows = close_branch(head_out, gate_vals, head_gain[2], out_weights[2])
        updated = widened + first_rows.astype(jnp.float32) + second_rows.astype(jnp.float32) + third_rows.astype(jnp.float32)
        trans_in = normalize(updated, trans_gain).astype(jnp.bfloat16)
        hidden = jax.nn.silu(jnp.dot(trans_in.reshape(-1, D), up_weight, preferred_element_type=jnp.float32)).astype(jnp.bfloat16)
        lowered = jnp.dot(hidden, down_weight, preferred_element_type=jnp.float32).reshape(updated.shape)
        return (updated + lowered).astype(jnp.bfloat16)
    result = lax.map(second_pass, (blocks, first_out, second_out))
    return result.reshape(ROWS, COLS, D)
```

```python
import jax
import jax.numpy as jnp
from jax import lax
from jax.experimental import pallas as pl
from jax.experimental.pallas import tpu as pltpu
from jax.sharding import PartitionSpec as P

D = 128
HEADS = 4
HEAD = 32
FF = 512
N_ROW = 16
N_COL = 16
ROW_DEV = 4
CHUNKS = 2
CHUNK = 16
EPS = 1e-05
MESH = pl.DeviceIdType.MESH
F32 = jnp.float32
BF16 = jnp.bfloat16

ROW_STEPS = [
    (1, 4), (0, 4), (1, 3), (1, 5), (0, 3), (0, 5), (1, 2), (1, 6),
    (0, 2), (0, 6), (1, 1), (1, 7), (0, 1), (0, 7), (1, 0),
]
COL_STEPS = [
    (dx, dl, dc) for dx in (2, 1, 3, 0) for dl in (1, 0) for dc in (1, 0) if (dx, dl, dc) != (0, 0, 0)
]


def dot(a, b):
    return jnp.dot(a, b, preferred_element_type=F32)


def dot_t(a, b):
    return lax.dot_general(a, b, (((1,), (1,)), ((), ())), preferred_element_type=F32)


def feature(v):
    return jnp.maximum(v, 0.0) + jnp.exp(jnp.minimum(v, 0.0))


def sigmoid(v):
    return 0.5 * jnp.tanh(0.5 * v) + 0.5


def normalize(v, gain):
    meansq = jnp.mean(v * v, axis=-1, keepdims=True)
    return v * lax.rsqrt(meansq + EPS) * gain


def same_head(rows, columns):
    r = lax.broadcasted_iota(jnp.int32, (rows, columns), 0) % D // HEAD
    c = lax.broadcasted_iota(jnp.int32, (rows, columns), 1) % D // HEAD
    return r == c


def kernel(
    x_hbm, ng_hbm, win_hbm, hg_hbm, wout_hbm, tg_hbm, up_hbm, down_hbm,
    out_ref,
    x, ng, win, hg, wout, tg, up, down,
    wkt, q_keep, gate_keep, upd,
    part, part_in, state, col_in, col_norm, col_res, col_out, ret,
    local_sem, f_send, f_recv, r_send, r_recv, own_sem, s_send, s_recv, g_send, g_recv,
):
    row = lax.axis_index("row")
    col = lax.axis_index("col")
    y_hi, z = row // 8, row % 8
    cx, cl, cc = col // 4, (col // 2) % 2, col % 2

    def row_peer(step):
        return ((y_hi + step[0]) % 2) * 8 + (z + step[1]) % 8

    def col_peer(step):
        return ((cx + step[0]) % 4) * 4 + ((cl + step[1]) % 2) * 2 + (cc + step[2]) % 2

    loads = [
        pltpu.make_async_copy(src, dst, local_sem.at[k])
        for k, (src, dst) in enumerate(
            [
                (x_hbm, x), (ng_hbm, ng), (win_hbm, win), (hg_hbm, hg),
                (wout_hbm, wout), (tg_hbm, tg), (up_hbm, up), (down_hbm, down),
            ]
        )
    ]
    for load in loads:
        load.start()
    own_in = [
        pltpu.make_async_copy(x_hbm.at[:, row, h], col_in.at[h, row], own_sem.at[h])
        for h in range(CHUNKS)
    ]
    for copy in own_in:
        copy.start()

    barrier = pltpu.get_barrier_semaphore()
    for step in ROW_STEPS:
        pl.semaphore_signal(barrier, 1, device_id=(row_peer(step), col), device_id_type=MESH)
    for step in COL_STEPS:
        pl.semaphore_signal(barrier, 1, device_id=(row, col_peer(step)), device_id_type=MESH)
    pl.semaphore_wait(barrier, len(ROW_STEPS) + len(COL_STEPS))

    sends = []
    for h in range(CHUNKS):
        for k, step in enumerate(ROW_STEPS):
            peer = row_peer(step)
            copy = pltpu.make_async_remote_copy(
                src_ref=x_hbm.at[:, peer, h],
                dst_ref=col_in.at[h, row],
                send_sem=f_send.at[h, k],
                recv_sem=f_recv.at[h, k],
                device_id=(peer, col),
                device_id_type=MESH,
            )
            copy.start()
            sends.append(copy)
    forward = [sends[: len(ROW_STEPS)], sends[len(ROW_STEPS) :]]

    for load in loads:
        load.wait()
    for p in range(3):
        wkt[p] = win[p, :, D : 2 * D].astype(F32).T.astype(BF16)

    head_mask = same_head(D, D)

    def row_open(i, carry):
        normed = normalize(x[i].reshape(512, D).astype(F32), ng[...]).astype(BF16)
        for p in range(2):
            q_keep[p, i] = feature(dot(normed, win[p, :, :D])).astype(BF16)
            key_t = feature(dot_t(wkt[p], normed)).astype(BF16)
            tail = dot(normed, win[p, :, 2 * D :])
            gate_keep[p, i] = sigmoid(tail[:, D:])
            full = dot(key_t, tail[:, :D].astype(BF16))
            full = jnp.where(head_mask, full, 0.0).reshape(HEADS, HEAD, D).sum(axis=0)
            part[p, i] = full.astype(BF16)
        return carry

    lax.fori_loop(0, ROW_DEV, row_open, 0)

    def slice_of(ref, at):
        return ref.at[at // 8, (at // 2) % 4, pl.ds((at % 2) * 16, 16)]

    scatter = []
    for k, step in enumerate(COL_STEPS):
        peer = col_peer(step)
        copy = pltpu.make_async_remote_copy(
            src_ref=slice_of(part, peer),
            dst_ref=part_in.at[col],
            send_sem=s_send.at[k],
            recv_sem=s_recv.at[k],
            device_id=(row, peer),
            device_id_type=MESH,
        )
        copy.start()
        scatter.append(copy)
    part_in[col] = slice_of(part, col)[...]
    for copy in scatter:
        copy.wait_recv()
    total = part_in[...].astype(F32).sum(axis=0)
    slice_of(state, col)[...] = total.astype(BF16)
    gather = []
    for k, step in enumerate(COL_STEPS):
        peer = col_peer(step)
        copy = pltpu.make_async_remote_copy(
            src_ref=slice_of(state, col),
            dst_ref=slice_of(state, col),
            send_sem=g_send.at[k],
            recv_sem=g_recv.at[k],
            device_id=(row, peer),
            device_id_type=MESH,
        )
        copy.start()
        gather.append(copy)

    first_half = lax.broadcasted_iota(jnp.int32, (D, D), 0) < 64
    pair_mask = same_head(D, 2 * D)

    def column_pass(h):
        own_in[h].wait()
        for copy in forward[h]:
            copy.wait_recv()
        for t in range(4):
            block = col_in[h, 4 * t : 4 * t + 4].reshape(256, D).astype(F32)
            col_norm[256 * t : 256 * t + 256, :] = normalize(block, ng[...])
        for group in range(4):
            normed = jnp.concatenate(
                [col_norm[pl.ds(4 * group + c, 64, stride=CHUNK), :] for c in range(4)], axis=0
            ).astype(BF16)
            query = feature(dot(normed, win[2, :, :D])).astype(BF16)
            key_t = feature(dot_t(wkt[2], normed)).astype(BF16)
            tail = dot(normed, win[2, :, 2 * D :])
            value = tail[:, :D].astype(BF16)
            heads = []
            for pair in range(2):
                at = slice(D * pair, D * pair + D)
                v = value[at]
                zero = jnp.zeros_like(v)
                v2 = jnp.concatenate(
                    [jnp.where(first_half, v, zero), jnp.where(first_half, zero, v)], axis=1
                )
                s = jnp.where(pair_mask, dot(key_t[:, at], v2), 0.0).astype(BF16)
                o = dot(query[at], s)
                heads += [o[:64, :D], o[64:, D:]]
            mixed = normalize(jnp.concatenate(heads, axis=0), hg[2:3]) * sigmoid(tail[:, D:])
            res = dot(mixed.astype(BF16), wout[2])
            for c in range(4):
                col_res[pl.ds(4 * group + c, 64, stride=CHUNK), :] = res[64 * c : 64 * c + 64]
        for t in range(4):
            col_out[h, 4 * t : 4 * t + 4] = (
                col_res[256 * t : 256 * t + 256, :].astype(BF16).reshape(4, ROW_DEV, CHUNK, D)
            )
        copies = []
        for k, step in enumerate(ROW_STEPS):
            peer = row_peer(step)
            copy = pltpu.make_async_remote_copy(
                src_ref=col_out.at[h, peer],
                dst_ref=ret.at[h, row],
                send_sem=r_send.at[h, k],
                recv_sem=r_recv.at[h, k],
                device_id=(peer, col),
                device_id_type=MESH,
            )
            copy.start()
            copies.append(copy)
        ret[h, row] = col_out[h, row]
        return copies

    back = [column_pass(0)]

    for copy in gather:
        copy.wait_recv()

    def row_close(i, carry):
        acc = x[i].reshape(512, D).astype(F32)
        for p in range(2):
            s = state[p, i]
            s = jnp.concatenate([s, s, s, s], axis=0)
            s = jnp.where(head_mask, s, jnp.zeros_like(s))
            mixed = normalize(dot(q_keep[p, i], s), hg[p : p + 1]) * gate_keep[p, i]
            acc = acc + dot(mixed.astype(BF16), wout[p]).astype(BF16).astype(F32)
        upd[i] = acc.reshape(N_ROW, CHUNKS, CHUNK, D)
        return carry

    lax.fori_loop(0, ROW_DEV, row_close, 0)

    back.append(column_pass(1))

    for h in range(CHUNKS):
        for copy in back[h]:
            copy.wait_recv()

        def transition(i, carry):
            u = (upd[i, :, h] + ret[h, :, i].astype(F32)).reshape(256, D)
            t = normalize(u, tg[...]).astype(BF16)
            hid = dot(t, up[...])
            hid = (hid * sigmoid(hid)).astype(BF16)
            out_ref[i, :, h] = (u + dot(hid, down[...])).astype(BF16).reshape(N_ROW, CHUNK, D)
            return carry

        lax.fori_loop(0, ROW_DEV, transition, 0)

    for copy in sends + scatter + gather + back[0] + back[1]:
        copy.wait_send()


def shards(x, norm_gain, in_weights, head_gain, out_weights, trans_gain, up_weight, down_weight):
    any_spec = pl.BlockSpec(memory_space=pl.ANY)
    n, m = len(ROW_STEPS), len(COL_STEPS)
    dma = pltpu.SemaphoreType.DMA
    out = pl.pallas_call(
        kernel,
        out_shape=jax.ShapeDtypeStruct((ROW_DEV, N_ROW, CHUNKS, CHUNK, D), BF16),
        in_specs=[any_spec] * 8,
        out_specs=pl.BlockSpec(memory_space=pltpu.VMEM),
        scratch_shapes=[
            pltpu.VMEM((ROW_DEV, N_ROW, CHUNKS, CHUNK, D), BF16),
            pltpu.VMEM((1, D), F32),
            pltpu.VMEM((3, D, 4 * D), BF16),
            pltpu.VMEM((3, D), F32),
            pltpu.VMEM((3, D, D), BF16),
            pltpu.VMEM((1, D), F32),
            pltpu.VMEM((D, FF), BF16),
            pltpu.VMEM((FF, D), BF16),
            pltpu.VMEM((3, D, D), BF16),
            pltpu.VMEM((2, ROW_DEV, 512, D), BF16),
            pltpu.VMEM((2, ROW_DEV, 512, D), F32),
            pltpu.VMEM((ROW_DEV, N_ROW, CHUNKS, CHUNK, D), F32),
            pltpu.VMEM((2, ROW_DEV, HEAD, D), BF16),
            pltpu.VMEM((N_COL, 16, D), BF16),
            pltpu.VMEM((2, ROW_DEV, HEAD, D), BF16),
            pltpu.VMEM((CHUNKS, N_ROW, ROW_DEV, CHUNK, D), BF16),
            pltpu.VMEM((64 * CHUNK, D), F32),
            pltpu.VMEM((64 * CHUNK, D), F32),
            pltpu.VMEM((CHUNKS, N_ROW, ROW_DEV, CHUNK, D), BF16),
            pltpu.VMEM((CHUNKS, N_ROW, ROW_DEV, CHUNK, D), BF16),
            dma((8,)), dma((CHUNKS, n)), dma((CHUNKS, n)), dma((CHUNKS, n)), dma((CHUNKS, n)),
            dma((CHUNKS,)), dma((m,)), dma((m,)), dma((m,)), dma((m,)),
        ],
        compiler_params=pltpu.CompilerParams(
            collective_id=0, has_side_effects=True, vmem_limit_bytes=60 * 1024 * 1024
        ),
    )(
        x.reshape(ROW_DEV, N_ROW, CHUNKS, CHUNK, D), norm_gain.reshape(1, D), in_weights, head_gain,
        out_weights, trans_gain.reshape(1, D), up_weight, down_weight,
    )
    return out.reshape(x.shape)


def solution(mesh):
    in_specs = (P("row", "col", None), P(), P(), P(), P(), P(), P(), P())
    return jax.shard_map(
        shards, mesh=mesh, in_specs=in_specs, out_specs=P("row", "col", None), check_vma=False
    )
```

```python
import jax
import jax.numpy as jnp
from jax import lax
from jax.experimental import pallas as pl
from jax.experimental.pallas import tpu as pltpu
from jax.sharding import PartitionSpec as P

D = 128
HEADS = 4
HEAD = 32
FF = 512
N_ROW = 16
N_COL = 16
ROW_DEV = 4
CHUNKS = 2
CHUNK = 16
EPS = 1e-05
MESH = pl.DeviceIdType.MESH
F32 = jnp.float32
BF16 = jnp.bfloat16

ROW_STEPS = [
    (1, 4), (0, 4), (1, 3), (1, 5), (0, 3), (0, 5), (1, 2), (1, 6),
    (0, 2), (0, 6), (1, 1), (1, 7), (0, 1), (0, 7), (1, 0),
]
COL_STEPS = [
    (dx, dl, dc) for dx in (2, 1, 3, 0) for dl in (1, 0) for dc in (1, 0) if (dx, dl, dc) != (0, 0, 0)
]


def arrived(ref, sem):
    pltpu.make_async_copy(ref, ref, sem).wait()


def dot(a, b):
    return jnp.dot(a, b, preferred_element_type=F32)


def dot_t(a, b):
    return lax.dot_general(a, b, (((1,), (1,)), ((), ())), preferred_element_type=F32)


def feature(v):
    return jnp.maximum(v, 0.0) + jnp.exp(jnp.minimum(v, 0.0))


def sigmoid(v):
    return 0.5 * jnp.tanh(0.5 * v) + 0.5


def normalize(v, gain):
    meansq = jnp.mean(v * v, axis=-1, keepdims=True)
    return v * lax.rsqrt(meansq + EPS) * gain


def same_head(rows, columns):
    r = lax.broadcasted_iota(jnp.int32, (rows, columns), 0) % D // HEAD
    c = lax.broadcasted_iota(jnp.int32, (rows, columns), 1) % D // HEAD
    return r == c


def kernel(
    x_hbm, ng_hbm, win_hbm, hg_hbm, wout_hbm, tg_hbm, up_hbm, down_hbm,
    out_ref,
    x, ng, win, hg, wout, tg, up, down,
    wkt, q_keep, gate_keep, upd,
    part, part_in, state, col_in, col_norm, col_res, col_out, ret,
    local_sem, f_send, f_recv, r_send, r_recv, s_send, s_recv, g_send, g_recv,
):
    row = lax.axis_index("row")
    col = lax.axis_index("col")
    y_hi, z = row // 8, row % 8
    cx, cl, cc = col // 4, (col // 2) % 2, col % 2

    def row_peer(step):
        return ((y_hi + step[0]) % 2) * 8 + (z + step[1]) % 8

    def col_peer(step):
        return ((cx + step[0]) % 4) * 4 + ((cl + step[1]) % 2) * 2 + (cc + step[2]) % 2

    loads = [
        pltpu.make_async_copy(src, dst, local_sem.at[int(k > 0)])
        for k, (src, dst) in enumerate(
            [
                (x_hbm, x), (ng_hbm, ng), (win_hbm, win), (hg_hbm, hg),
                (wout_hbm, wout), (tg_hbm, tg), (up_hbm, up), (down_hbm, down),
            ]
        )
    ]
    for load in loads:
        load.start()
    for h in range(CHUNKS):
        pltpu.make_async_copy(x_hbm.at[:, row, h], col_in.at[h, row], f_recv.at[h]).start()

    barrier = pltpu.get_barrier_semaphore()
    for step in ROW_STEPS:
        pl.semaphore_signal(barrier, 1, device_id=(row_peer(step), col), device_id_type=MESH)
    for step in COL_STEPS:
        pl.semaphore_signal(barrier, 1, device_id=(row, col_peer(step)), device_id_type=MESH)
    with jax.named_scope('bar'):
        pl.semaphore_wait(barrier, len(ROW_STEPS) + len(COL_STEPS))

    for h in range(CHUNKS):
        for step in ROW_STEPS:
            peer = row_peer(step)
            pltpu.make_async_remote_copy(
                src_ref=x_hbm.at[:, peer, h],
                dst_ref=col_in.at[h, row],
                send_sem=f_send,
                recv_sem=f_recv.at[h],
                device_id=(peer, col),
                device_id_type=MESH,
            ).start()

    with jax.named_scope("loads"):
      for load in loads:
        load.wait()
    for p in range(3):
        wkt[p] = win[p, :, D : 2 * D].astype(F32).T.astype(BF16)

    head_mask = same_head(D, D)

    def row_open(i, carry):
        normed = normalize(x[i].reshape(512, D).astype(F32), ng[...]).astype(BF16)
        for p in range(2):
            q_keep[p, i] = feature(dot(normed, win[p, :, :D])).astype(BF16)
            key_t = feature(dot_t(wkt[p], normed)).astype(BF16)
            tail = dot(normed, win[p, :, 2 * D :])
            gate_keep[p, i] = sigmoid(tail[:, D:])
            full = dot(key_t, tail[:, :D].astype(BF16))
            full = jnp.where(head_mask, full, 0.0).reshape(HEADS, HEAD, D).sum(axis=0)
            part[p, i] = full.astype(BF16)
        return carry

    with jax.named_scope('row_open'):
        lax.fori_loop(0, ROW_DEV, row_open, 0, unroll=True)

    def slice_of(ref, at):
        return ref.at[at // 8, (at // 2) % 4, pl.ds((at % 2) * 16, 16)]

    for step in COL_STEPS:
        peer = col_peer(step)
        pltpu.make_async_remote_copy(
            src_ref=slice_of(part, peer),
            dst_ref=part_in.at[col],
            send_sem=s_send,
            recv_sem=s_recv,
            device_id=(row, peer),
            device_id_type=MESH,
        ).start()
    part_in[col] = slice_of(part, col)[...]
    with jax.named_scope("rs_wait"):
        arrived(part_in.at[: N_COL - 1], s_recv)
    total = part_in[...].astype(F32).sum(axis=0)
    slice_of(state, col)[...] = total.astype(BF16)
    for step in COL_STEPS:
        peer = col_peer(step)
        pltpu.make_async_remote_copy(
            src_ref=slice_of(state, col),
            dst_ref=slice_of(state, col),
            send_sem=g_send,
            recv_sem=g_recv,
            device_id=(row, peer),
            device_id_type=MESH,
        ).start()

    first_half = lax.broadcasted_iota(jnp.int32, (D, D), 0) < 64
    pair_mask = same_head(D, 2 * D)

    def column_pass(h):
        with jax.named_scope("f_wait"):
            arrived(col_in.at[h], f_recv.at[h])
        for t in range(4):
            block = col_in[h, 4 * t : 4 * t + 4].reshape(256, D).astype(F32)
            col_norm[256 * t : 256 * t + 256, :] = normalize(block, ng[...])
        for group in range(4):
            normed = jnp.concatenate(
                [col_norm[pl.ds(4 * group + c, 64, stride=CHUNK), :] for c in range(4)], axis=0
            ).astype(BF16)
            query = feature(dot(normed, win[2, :, :D])).astype(BF16)
            key_t = feature(dot_t(wkt[2], normed)).astype(BF16)
            tail = dot(normed, win[2, :, 2 * D :])
            value = tail[:, :D].astype(BF16)
            heads = []
            for pair in range(2):
                at = slice(D * pair, D * pair + D)
                v = value[at]
                zero = jnp.zeros_like(v)
                v2 = jnp.concatenate(
                    [jnp.where(first_half, v, zero), jnp.where(first_half, zero, v)], axis=1
                )
                s = jnp.where(pair_mask, dot(key_t[:, at], v2), 0.0).astype(BF16)
                o = dot(query[at], s)
                heads += [o[:64, :D], o[64:, D:]]
            mixed = normalize(jnp.concatenate(heads, axis=0), hg[2:3]) * sigmoid(tail[:, D:])
            res = dot(mixed.astype(BF16), wout[2])
            for c in range(4):
                col_res[pl.ds(4 * group + c, 64, stride=CHUNK), :] = res[64 * c : 64 * c + 64]
        for t in range(4):
            col_out[h, 4 * t : 4 * t + 4] = (
                col_res[256 * t : 256 * t + 256, :].astype(BF16).reshape(4, ROW_DEV, CHUNK, D)
            )
        for half in range(2):
            rows = pl.ds(2 * half, 2)
            for step in ROW_STEPS:
                peer = row_peer(step)
                pltpu.make_async_remote_copy(
                    src_ref=col_out.at[h, peer, rows],
                    dst_ref=ret.at[h, row, rows],
                    send_sem=r_send,
                    recv_sem=r_recv.at[h, half],
                    device_id=(peer, col),
                    device_id_type=MESH,
                ).start()
        ret[h, row] = col_out[h, row]

    with jax.named_scope("col_a"):
        column_pass(0)

    with jax.named_scope("ag_wait"):
        arrived(part_in.at[: N_COL - 1], g_recv)

    def row_close(i, carry):
        acc = x[i].reshape(512, D).astype(F32)
        for p in range(2):
            s = state[p, i]
            s = jnp.concatenate([s, s, s, s], axis=0)
            s = jnp.where(head_mask, s, jnp.zeros_like(s))
            mixed = normalize(dot(q_keep[p, i], s), hg[p : p + 1]) * gate_keep[p, i]
            acc = acc + dot(mixed.astype(BF16), wout[p]).astype(BF16).astype(F32)
        upd[i] = acc.reshape(N_ROW, CHUNKS, CHUNK, D)
        return carry

    with jax.named_scope('row_close'):
        lax.fori_loop(0, ROW_DEV, row_close, 0, unroll=True)

    with jax.named_scope('col_b'):
        column_pass(1)

    for h in range(CHUNKS):
        for half in range(2):
            with jax.named_scope("r_wait"):
                arrived(ret.at[h, : N_ROW - 1, pl.ds(2 * half, 2)], r_recv.at[h, half])
            with jax.named_scope("trans"):
                for i in (2 * half, 2 * half + 1):
                    u = (upd[i, :, h] + ret[h, :, i].astype(F32)).reshape(256, D)
                    t = normalize(u, tg[...]).astype(BF16)
                    hid = dot(t, up[...])
                    hid = (hid * sigmoid(hid)).astype(BF16)
                    out_ref[i, :, h] = (u + dot(hid, down[...])).astype(BF16).reshape(N_ROW, CHUNK, D)

    arrived(col_in.at[:, : N_ROW - 1], f_send)
    arrived(part_in.at[: N_COL - 1], s_send)
    arrived(part_in.at[: N_COL - 1], g_send)
    arrived(col_out.at[:, : N_ROW - 1], r_send)


def shards(x, norm_gain, in_weights, head_gain, out_weights, trans_gain, up_weight, down_weight):
    any_spec = pl.BlockSpec(memory_space=pltpu.HBM)
    dma = pltpu.SemaphoreType.DMA
    out = pl.pallas_call(
        kernel,
        out_shape=pltpu.VMEM((ROW_DEV, N_ROW, CHUNKS, CHUNK, D), BF16),
        in_specs=[any_spec] * 8,
        out_specs=pl.BlockSpec(memory_space=pltpu.VMEM),
        scratch_shapes=[
            pltpu.VMEM((ROW_DEV, N_ROW, CHUNKS, CHUNK, D), BF16),
            pltpu.VMEM((1, D), F32),
            pltpu.VMEM((3, D, 4 * D), BF16),
            pltpu.VMEM((3, D), F32),
            pltpu.VMEM((3, D, D), BF16),
            pltpu.VMEM((1, D), F32),
            pltpu.VMEM((D, FF), BF16),
            pltpu.VMEM((FF, D), BF16),
            pltpu.VMEM((3, D, D), BF16),
            pltpu.VMEM((2, ROW_DEV, 512, D), BF16),
            pltpu.VMEM((2, ROW_DEV, 512, D), F32),
            pltpu.VMEM((ROW_DEV, N_ROW, CHUNKS, CHUNK, D), F32),
            pltpu.VMEM((2, ROW_DEV, HEAD, D), BF16),
            pltpu.VMEM((N_COL, 16, D), BF16),
            pltpu.VMEM((2, ROW_DEV, HEAD, D), BF16),
            pltpu.VMEM((CHUNKS, N_ROW, ROW_DEV, CHUNK, D), BF16),
            pltpu.VMEM((64 * CHUNK, D), F32),
            pltpu.VMEM((64 * CHUNK, D), F32),
            pltpu.VMEM((CHUNKS, N_ROW, ROW_DEV, CHUNK, D), BF16),
            pltpu.VMEM((CHUNKS, N_ROW, ROW_DEV, CHUNK, D), BF16),
            dma((2,)), dma(()), dma((CHUNKS,)), dma(()), dma((CHUNKS, 2)),
            dma(()), dma(()), dma(()), dma(()),
        ],
        compiler_params=pltpu.CompilerParams(
            collective_id=0, has_side_effects=True, vmem_limit_bytes=60 * 1024 * 1024
        ),
    )(
        x.reshape(ROW_DEV, N_ROW, CHUNKS, CHUNK, D), norm_gain.reshape(1, D), in_weights, head_gain,
        out_weights, trans_gain.reshape(1, D), up_weight, down_weight,
    )
    return out.reshape(x.shape)


def solution(mesh):
    in_specs = (P("row", "col", None), P(), P(), P(), P(), P(), P(), P())
    return jax.shard_map(
        shards, mesh=mesh, in_specs=in_specs, out_specs=P("row", "col", None), check_vma=False
    )
```

```python
import jax
import jax.numpy as jnp
from jax import lax
from jax.experimental import pallas as pl
from jax.experimental.pallas import tpu as pltpu
from jax.sharding import PartitionSpec as P

D = 128
HEADS = 4
HEAD = 32
FF = 512
N_ROW = 16
N_COL = 16
ROW_DEV = 4
UNITS = 4
UNIT = 8
FORWARD = [(0, 1), (1, 2), (2, 3), (3, 4)]
BACK = [[((0, 1), (0, 4)), ((1, 2), (0, 4))], [((2, 3), (0, 4)), ((3, 4), (0, 2)), ((3, 4), (2, 4))]]
EPS = 1e-05
MESH = pl.DeviceIdType.MESH
F32 = jnp.float32
BF16 = jnp.bfloat16

ROW_STAGES = [
    [(0, 2), (0, 6), (0, 1), (0, 7), (1, 0)],
    [(0, 4), (0, 3), (0, 5), (1, 2), (1, 6), (1, 1), (1, 7)],
    [(1, 4), (1, 3), (1, 5)],
]
ROW_STEPS = [step for stage in ROW_STAGES[::-1] for step in stage]
COL_STEPS = [
    (dx, dl, dc) for dx in (2, 1, 3, 0) for dl in (1, 0) for dc in (1, 0) if (dx, dl, dc) != (0, 0, 0)
]
FILL = ([(k, step) for k in (1, 2, 3) for step in ROW_STAGES[0][:4]], [])
COL_NEXT = [(1, 0, 0), (3, 0, 0), (0, 1, 0), (0, 0, 1)]


def arrived(ref, sem):
    pltpu.make_async_copy(ref, ref, sem).wait()


def dot(a, b):
    return jnp.dot(a, b, preferred_element_type=F32)


def dot_t(a, b):
    return lax.dot_general(a, b, (((1,), (1,)), ((), ())), preferred_element_type=F32)


def feature(v):
    return jnp.maximum(v, 0.0) + jnp.exp(jnp.minimum(v, 0.0))


def sigmoid(v):
    return 0.5 * jnp.tanh(0.5 * v) + 0.5


def normalize(v, gain):
    meansq = jnp.mean(v * v, axis=-1, keepdims=True)
    return v * lax.rsqrt(meansq + EPS) * gain


def same_head(rows, columns):
    r = lax.broadcasted_iota(jnp.int32, (rows, columns), 0) % D // HEAD
    c = lax.broadcasted_iota(jnp.int32, (rows, columns), 1) % D // HEAD
    return r == c


def kernel(
    x_hbm, ng_hbm, win_hbm, hg_hbm, wout_hbm, tg_hbm, up_hbm, down_hbm,
    out_ref,
    x, ng, win, hg, wout, tg, up, down,
    wkt, q_keep, gate_keep, upd,
    part, part_in, state, col_in, col_norm, col_res, col_out, ret,
    local_sem, f_send, f_recv, r_send, r_recv, s_send, s_recv, g_send, g_recv, row_in, col_told,
):
    row = lax.axis_index("row")
    col = lax.axis_index("col")
    y_hi, z = row // 8, row % 8
    cx, cl, cc = col // 4, (col // 2) % 2, col % 2

    def row_peer(step):
        return ((y_hi + step[0]) % 2) * 8 + (z + step[1]) % 8

    def col_peer(step):
        return ((cx + step[0]) % 4) * 4 + ((cl + step[1]) % 2) * 2 + (cc + step[2]) % 2

    loads = [
        pltpu.make_async_copy(src, dst, local_sem.at[int(k > 0)])
        for k, (src, dst) in enumerate(
            [
                (x_hbm, x), (ng_hbm, ng), (win_hbm, win), (hg_hbm, hg),
                (wout_hbm, wout), (tg_hbm, tg), (up_hbm, up), (down_hbm, down),
            ]
        )
    ]
    for load in loads:
        load.start()
    for k, (u0, u1) in enumerate(FORWARD):
        units = pl.ds(u0, u1 - u0)
        pltpu.make_async_copy(
            x_hbm.at[:, row, units], col_in.at[row, :, units], f_recv.at[k]
        ).start()

    def send_forward(k, step):
        peer = row_peer(step)
        units = pl.ds(FORWARD[k][0], FORWARD[k][1] - FORWARD[k][0])
        pltpu.make_async_remote_copy(
            src_ref=x_hbm.at[:, peer, units],
            dst_ref=col_in.at[row, :, units],
            send_sem=f_send,
            recv_sem=f_recv.at[k],
            device_id=(peer, col),
            device_id_type=MESH,
        ).start()

    def tell_row(sem, steps):
        for step in steps:
            pl.semaphore_signal(sem, 1, device_id=(row_peer(step), col), device_id_type=MESH)

    def tell_col(sem):
        for step in COL_NEXT:
            pl.semaphore_signal(sem, 1, device_id=(row, col_peer(step)), device_id_type=MESH)

    barrier = pltpu.get_barrier_semaphore()
    tell_row(barrier, ROW_STAGES[0])
    tell_col(barrier)
    with jax.named_scope("bar"):
        pl.semaphore_wait(barrier, len(ROW_STAGES[0]) + len(COL_NEXT))
    near = ROW_STAGES[0][:4]
    tell_row(row_in.at[0], near)
    tell_col(col_told.at[0])
    for step in ROW_STAGES[0]:
        send_forward(0, step)
    for k, step in FILL[0]:
        send_forward(k, step)
    with jax.named_scope("stage"):
        pl.semaphore_wait(row_in.at[0], len(near))
    tell_row(row_in.at[1], [(1, 0)])
    for step in ROW_STAGES[1]:
        send_forward(0, step)
    for k, step in FILL[1]:
        send_forward(k, step)
    pl.semaphore_wait(col_told.at[0], len(COL_NEXT))
    tell_col(col_told.at[1])
    with jax.named_scope("stage"):
        pl.semaphore_wait(row_in.at[1], 1)
    for step in ROW_STAGES[2]:
        send_forward(0, step)
    for k in range(1, len(FORWARD)):
        for step in ROW_STEPS:
            if (k, step) not in FILL[0] + FILL[1]:
                send_forward(k, step)
    pl.semaphore_wait(col_told.at[1], len(COL_NEXT))
    tell_col(col_told.at[2])

    with jax.named_scope("loads"):
      for load in loads:
        load.wait()
    for p in range(3):
        wkt[p] = win[p, :, D : 2 * D].astype(F32).T.astype(BF16)

    head_mask = same_head(D, D)

    def row_open(i, carry):
        normed = normalize(x[i].reshape(512, D).astype(F32), ng[...]).astype(BF16)
        for p in range(2):
            q_keep[p, i] = feature(dot(normed, win[p, :, :D])).astype(BF16)
            key_t = feature(dot_t(wkt[p], normed)).astype(BF16)
            tail = dot(normed, win[p, :, 2 * D :])
            gate_keep[p, i] = sigmoid(tail[:, D:])
            full = dot(key_t, tail[:, :D].astype(BF16))
            full = jnp.where(head_mask, full, 0.0).reshape(HEADS, HEAD, D).sum(axis=0)
            part[p, i] = full.astype(BF16)
        return carry

    with jax.named_scope('row_open'):
        lax.fori_loop(0, ROW_DEV, row_open, 0, unroll=True)
    pl.semaphore_wait(col_told.at[2], len(COL_NEXT))

    def slice_of(ref, at):
        return ref.at[at // 8, (at // 2) % 4, pl.ds((at % 2) * 16, 16)]

    for step in COL_STEPS:
        peer = col_peer(step)
        pltpu.make_async_remote_copy(
            src_ref=slice_of(part, peer),
            dst_ref=part_in.at[col],
            send_sem=s_send,
            recv_sem=s_recv,
            device_id=(row, peer),
            device_id_type=MESH,
        ).start()
    part_in[col] = slice_of(part, col)[...]

    first_half = lax.broadcasted_iota(jnp.int32, (D, D), 0) < 64
    pair_mask = same_head(D, 2 * D)

    def column_pass(u):
        block = col_in[:, :, u].reshape(64 * UNIT, D).astype(F32)
        col_norm[...] = normalize(block, ng[...])
        for group in range(UNIT // 4):
            normed = jnp.concatenate(
                [col_norm[pl.ds(4 * group + c, 64, stride=UNIT), :] for c in range(4)], axis=0
            ).astype(BF16)
            query = feature(dot(normed, win[2, :, :D])).astype(BF16)
            key_t = feature(dot_t(wkt[2], normed)).astype(BF16)
            tail = dot(normed, win[2, :, 2 * D :])
            value = tail[:, :D].astype(BF16)
            heads = []
            for pair in range(2):
                at = slice(D * pair, D * pair + D)
                v = value[at]
                zero = jnp.zeros_like(v)
                v2 = jnp.concatenate(
                    [jnp.where(first_half, v, zero), jnp.where(first_half, zero, v)], axis=1
                )
                s = jnp.where(pair_mask, dot(key_t[:, at], v2), 0.0).astype(BF16)
                o = dot(query[at], s)
                heads += [o[:64, :D], o[64:, D:]]
            mixed = normalize(jnp.concatenate(heads, axis=0), hg[2:3]) * sigmoid(tail[:, D:])
            res = dot(mixed.astype(BF16), wout[2])
            for c in range(4):
                col_res[pl.ds(4 * group + c, 64, stride=UNIT), :] = res[64 * c : 64 * c + 64]
        col_out[:, :, u] = col_res[...].astype(BF16).reshape(N_ROW, ROW_DEV, UNIT, D)

    groups = [group for groups in BACK for group in groups]

    def send_back(g):
        (u0, u1), (i0, i1) = groups[g]
        rows, units = pl.ds(i0, i1 - i0), pl.ds(u0, u1 - u0)
        for step in ROW_STEPS:
            peer = row_peer(step)
            pltpu.make_async_remote_copy(
                src_ref=col_out.at[peer, rows, units],
                dst_ref=ret.at[row, rows, units],
                send_sem=r_send,
                recv_sem=r_recv.at[g],
                device_id=(peer, col),
                device_id_type=MESH,
            ).start()

    def column_chunk(k):
        with jax.named_scope("f_wait"):
            arrived(col_in.at[:, :, pl.ds(FORWARD[k][0], FORWARD[k][1] - FORWARD[k][0])], f_recv.at[k])
        for u in range(*FORWARD[k]):
            with jax.named_scope("col_pass"):
                column_pass(u)
            for g, ((u0, u1), _) in enumerate(groups):
                if u1 == u + 1:
                    send_back(g)
            ret[row, :, u] = col_out[row, :, u]

    column_chunk(0)

    with jax.named_scope("rs_wait"):
        arrived(part_in.at[: N_COL - 1], s_recv)
    total = part_in[...].astype(F32).sum(axis=0)
    slice_of(state, col)[...] = total.astype(BF16)
    for step in COL_STEPS:
        peer = col_peer(step)
        pltpu.make_async_remote_copy(
            src_ref=slice_of(state, col),
            dst_ref=slice_of(state, col),
            send_sem=g_send,
            recv_sem=g_recv,
            device_id=(row, peer),
            device_id_type=MESH,
        ).start()

    for k in range(1, len(FORWARD)):
        column_chunk(k)

    with jax.named_scope("ag_wait"):
        arrived(part_in.at[: N_COL - 1], g_recv)

    def row_close(i, carry):
        acc = x[i].reshape(512, D).astype(F32)
        for p in range(2):
            s = state[p, i]
            s = jnp.concatenate([s, s, s, s], axis=0)
            s = jnp.where(head_mask, s, jnp.zeros_like(s))
            mixed = normalize(dot(q_keep[p, i], s), hg[p : p + 1]) * gate_keep[p, i]
            acc = acc + dot(mixed.astype(BF16), wout[p]).astype(BF16).astype(F32)
        upd[i] = acc.reshape(N_ROW, UNITS, UNIT, D)
        return carry

    with jax.named_scope('row_close'):
        lax.fori_loop(0, ROW_DEV, row_close, 0, unroll=True)

    for g, ((u0, u1), (i0, i1)) in enumerate(groups):
        with jax.named_scope("r_wait"):
            arrived(ret.at[: N_ROW - 1, pl.ds(i0, i1 - i0), pl.ds(u0, u1 - u0)], r_recv.at[g])
        with jax.named_scope("trans"):
            for u in range(u0, u1):
                for i in range(i0, i1, 2):
                    both = [upd[r, :, u] + ret[:, r, u].astype(F32) for r in (i, i + 1)]
                    v = jnp.concatenate(both, axis=0).reshape(2 * N_ROW * UNIT, D)
                    t = normalize(v, tg[...]).astype(BF16)
                    hid = dot(t, up[...])
                    hid = (hid * sigmoid(hid)).astype(BF16)
                    res = (v + dot(hid, down[...])).astype(BF16).reshape(2, N_ROW, UNIT, D)
                    out_ref[i, :, u] = res[0]
                    out_ref[i + 1, :, u] = res[1]

    arrived(col_in.at[: N_ROW - 1], f_send)
    arrived(part_in.at[: N_COL - 1], s_send)
    arrived(part_in.at[: N_COL - 1], g_send)
    arrived(col_out.at[: N_ROW - 1], r_send)


def shards(x, norm_gain, in_weights, head_gain, out_weights, trans_gain, up_weight, down_weight):
    any_spec = pl.BlockSpec(memory_space=pltpu.HBM)
    dma = pltpu.SemaphoreType.DMA
    out = pl.pallas_call(
        kernel,
        out_shape=pltpu.VMEM((ROW_DEV, N_ROW, UNITS, UNIT, D), BF16),
        in_specs=[any_spec] * 8,
        out_specs=pl.BlockSpec(memory_space=pltpu.VMEM),
        scratch_shapes=[
            pltpu.VMEM((ROW_DEV, N_ROW, UNITS, UNIT, D), BF16),
            pltpu.VMEM((1, D), F32),
            pltpu.VMEM((3, D, 4 * D), BF16),
            pltpu.VMEM((3, D), F32),
            pltpu.VMEM((3, D, D), BF16),
            pltpu.VMEM((1, D), F32),
            pltpu.VMEM((D, FF), BF16),
            pltpu.VMEM((FF, D), BF16),
            pltpu.VMEM((3, D, D), BF16),
            pltpu.VMEM((2, ROW_DEV, 512, D), BF16),
            pltpu.VMEM((2, ROW_DEV, 512, D), F32),
            pltpu.VMEM((ROW_DEV, N_ROW, UNITS, UNIT, D), F32),
            pltpu.VMEM((2, ROW_DEV, HEAD, D), BF16),
            pltpu.VMEM((N_COL, 16, D), BF16),
            pltpu.VMEM((2, ROW_DEV, HEAD, D), BF16),
            pltpu.VMEM((N_ROW, ROW_DEV, UNITS, UNIT, D), BF16),
            pltpu.VMEM((64 * UNIT, D), F32),
            pltpu.VMEM((64 * UNIT, D), F32),
            pltpu.VMEM((N_ROW, ROW_DEV, UNITS, UNIT, D), BF16),
            pltpu.VMEM((N_ROW, ROW_DEV, UNITS, UNIT, D), BF16),
            dma((2,)), dma(()), dma((len(FORWARD),)), dma(()), dma((sum(map(len, BACK)),)),
            dma(()), dma(()), dma(()), dma(()),
            pltpu.SemaphoreType.REGULAR((2,)), pltpu.SemaphoreType.REGULAR((3,)),
        ],
        compiler_params=pltpu.CompilerParams(
            collective_id=0, has_side_effects=True, vmem_limit_bytes=60 * 1024 * 1024
        ),
    )(
        x.reshape(ROW_DEV, N_ROW, UNITS, UNIT, D), norm_gain.reshape(1, D), in_weights, head_gain,
        out_weights, trans_gain.reshape(1, D), up_weight, down_weight,
    )
    return out.reshape(x.shape)


def solution(mesh):
    in_specs = (P("row", "col", None), P(), P(), P(), P(), P(), P(), P())
    return jax.shard_map(
        shards, mesh=mesh, in_specs=in_specs, out_specs=P("row", "col", None), check_vma=False
    )
```

```python
import jax
import jax.numpy as jnp
from jax import lax
from jax.experimental import pallas as pl
from jax.experimental.pallas import tpu as pltpu
from jax.sharding import PartitionSpec as P

D = 128
HEADS = 4
HEAD = 32
FF = 512
N_ROW = 16
N_COL = 16
ROW_DEV = 4
UNITS = 4
UNIT = 8
FORWARD = [(0, 1), (1, 2), (2, 3), (3, 4)]
BACK = [[((0, 1), (0, 4)), ((1, 2), (0, 4))], [((2, 3), (0, 4)), ((3, 4), (0, 2)), ((3, 4), (2, 4))]]
EPS = 1e-05
MESH = pl.DeviceIdType.MESH
F32 = jnp.float32
BF16 = jnp.bfloat16

ROW_STAGES = [
    [(0, 2), (0, 6), (0, 1), (0, 7), (1, 0)],
    [(0, 4), (0, 3), (0, 5), (1, 2), (1, 6), (1, 1), (1, 7)],
    [(1, 4), (1, 3), (1, 5)],
]
ROW_STEPS = [step for stage in ROW_STAGES[::-1] for step in stage]
FAR, NEAR = ROW_STEPS[:8], ROW_STEPS[8:]
ISSUE = [[(0, ROW_STEPS)], [(1, ROW_STEPS)], [(2, FAR)], [(3, FAR), (4, FAR), (2, NEAR), (3, NEAR), (4, NEAR)]]
COL_STEPS = [
    (dx, dl, dc) for dx in (2, 1, 3, 0) for dl in (1, 0) for dc in (1, 0) if (dx, dl, dc) != (0, 0, 0)
]
FILL = ([(k, step) for k in (1, 2, 3) for step in ROW_STAGES[0][:4]], [])
COL_NEXT = [(1, 0, 0), (3, 0, 0), (0, 1, 0), (0, 0, 1)]


def arrived(ref, sem):
    pltpu.make_async_copy(ref, ref, sem).wait()


def dot(a, b):
    return jnp.dot(a, b, preferred_element_type=F32)


def dot_t(a, b):
    return lax.dot_general(a, b, (((1,), (1,)), ((), ())), preferred_element_type=F32)


def feature(v):
    return jnp.maximum(v, 0.0) + jnp.exp(jnp.minimum(v, 0.0))


def sigmoid(v):
    return 0.5 * jnp.tanh(0.5 * v) + 0.5


def normalize(v, gain):
    meansq = jnp.mean(v * v, axis=-1, keepdims=True)
    return v * lax.rsqrt(meansq + EPS) * gain


def transition(v, tg, up, down):
    hid = dot(normalize(v, tg[...]).astype(BF16), up[...])
    hid = (hid * sigmoid(hid)).astype(BF16)
    return (v + dot(hid, down[...])).astype(BF16)


def same_head(rows, columns):
    r = lax.broadcasted_iota(jnp.int32, (rows, columns), 0) % D // HEAD
    c = lax.broadcasted_iota(jnp.int32, (rows, columns), 1) % D // HEAD
    return r == c


def kernel(
    x_hbm, ng_hbm, win_hbm, hg_hbm, wout_hbm, tg_hbm, up_hbm, down_hbm,
    out_ref, last, tg, up, down,
    x, ng, win, hg, wout,
    wkt, q_keep, gate_keep, upd,
    part, part_in, state, col_in, col_norm, col_res, col_out, ret,
    local_sem, f_send, f_recv, r_send, r_recv, s_send, s_recv, g_send, g_recv, row_in, col_told,
):
    row = lax.axis_index("row")
    col = lax.axis_index("col")
    y_hi, z = row // 8, row % 8
    cx, cl, cc = col // 4, (col // 2) % 2, col % 2

    def row_peer(step):
        return ((y_hi + step[0]) % 2) * 8 + (z + step[1]) % 8

    def col_peer(step):
        return ((cx + step[0]) % 4) * 4 + ((cl + step[1]) % 2) * 2 + (cc + step[2]) % 2

    loads = [
        pltpu.make_async_copy(src, dst, local_sem.at[int(k > 0)])
        for k, (src, dst) in enumerate(
            [
                (x_hbm, x), (ng_hbm, ng), (win_hbm, win), (hg_hbm, hg),
                (wout_hbm, wout), (tg_hbm, tg), (up_hbm, up), (down_hbm, down),
            ]
        )
    ]
    for load in loads:
        load.start()
    for k, (u0, u1) in enumerate(FORWARD):
        units = pl.ds(u0, u1 - u0)
        pltpu.make_async_copy(
            x_hbm.at[:, row, units], col_in.at[row, :, units], f_recv.at[k]
        ).start()

    def send_forward(k, step):
        peer = row_peer(step)
        units = pl.ds(FORWARD[k][0], FORWARD[k][1] - FORWARD[k][0])
        pltpu.make_async_remote_copy(
            src_ref=x_hbm.at[:, peer, units],
            dst_ref=col_in.at[row, :, units],
            send_sem=f_send,
            recv_sem=f_recv.at[k],
            device_id=(peer, col),
            device_id_type=MESH,
        ).start()

    def tell_row(sem, steps):
        for step in steps:
            pl.semaphore_signal(sem, 1, device_id=(row_peer(step), col), device_id_type=MESH)

    def tell_col(sem):
        for step in COL_NEXT:
            pl.semaphore_signal(sem, 1, device_id=(row, col_peer(step)), device_id_type=MESH)

    barrier = pltpu.get_barrier_semaphore()
    tell_row(barrier, ROW_STAGES[0])
    tell_col(barrier)
    with jax.named_scope("bar"):
        pl.semaphore_wait(barrier, len(ROW_STAGES[0]) + len(COL_NEXT))
    near = ROW_STAGES[0][:4]
    tell_row(row_in.at[0], near)
    tell_col(col_told.at[0])
    for step in ROW_STAGES[0]:
        send_forward(0, step)
    for k, step in FILL[0]:
        send_forward(k, step)
    with jax.named_scope("stage"):
        pl.semaphore_wait(row_in.at[0], len(near))
    tell_row(row_in.at[1], [(1, 0)])
    for step in ROW_STAGES[1]:
        send_forward(0, step)
    for k, step in FILL[1]:
        send_forward(k, step)
    pl.semaphore_wait(col_told.at[0], len(COL_NEXT))
    tell_col(col_told.at[1])
    with jax.named_scope("stage"):
        pl.semaphore_wait(row_in.at[1], 1)
    for step in ROW_STAGES[2]:
        send_forward(0, step)
    for k in range(1, len(FORWARD)):
        for step in ROW_STEPS:
            if (k, step) not in FILL[0] + FILL[1]:
                send_forward(k, step)
    pl.semaphore_wait(col_told.at[1], len(COL_NEXT))
    tell_col(col_told.at[2])

    with jax.named_scope("loads"):
      for load in loads:
        load.wait()
    for p in range(3):
        wkt[p] = win[p, :, D : 2 * D].astype(F32).T.astype(BF16)

    head_mask = same_head(D, D)

    def row_open(i, carry):
        normed = normalize(x[i].reshape(512, D).astype(F32), ng[...]).astype(BF16)
        for p in range(2):
            q_keep[p, i] = feature(dot(normed, win[p, :, :D])).astype(BF16)
            key_t = feature(dot_t(wkt[p], normed)).astype(BF16)
            tail = dot(normed, win[p, :, 2 * D :])
            gate_keep[p, i] = sigmoid(tail[:, D:])
            full = dot(key_t, tail[:, :D].astype(BF16))
            full = jnp.where(head_mask, full, 0.0).reshape(HEADS, HEAD, D).sum(axis=0)
            part[p, i] = full.astype(BF16)
        return carry

    with jax.named_scope('row_open'):
        lax.fori_loop(0, ROW_DEV, row_open, 0, unroll=True)
    pl.semaphore_wait(col_told.at[2], len(COL_NEXT))

    def slice_of(ref, at):
        return ref.at[at // 8, (at // 2) % 4, pl.ds((at % 2) * 16, 16)]

    for step in COL_STEPS:
        peer = col_peer(step)
        pltpu.make_async_remote_copy(
            src_ref=slice_of(part, peer),
            dst_ref=part_in.at[col],
            send_sem=s_send,
            recv_sem=s_recv,
            device_id=(row, peer),
            device_id_type=MESH,
        ).start()
    part_in[col] = slice_of(part, col)[...]

    first_half = lax.broadcasted_iota(jnp.int32, (D, D), 0) < 64
    pair_mask = same_head(D, 2 * D)

    def column_pass(u):
        block = col_in[:, :, u].reshape(64 * UNIT, D).astype(F32)
        col_norm[...] = normalize(block, ng[...])
        for group in range(UNIT // 4):
            normed = jnp.concatenate(
                [col_norm[pl.ds(4 * group + c, 64, stride=UNIT), :] for c in range(4)], axis=0
            ).astype(BF16)
            query = feature(dot(normed, win[2, :, :D])).astype(BF16)
            key_t = feature(dot_t(wkt[2], normed)).astype(BF16)
            tail = dot(normed, win[2, :, 2 * D :])
            value = tail[:, :D].astype(BF16)
            heads = []
            for pair in range(2):
                at = slice(D * pair, D * pair + D)
                v = value[at]
                zero = jnp.zeros_like(v)
                v2 = jnp.concatenate(
                    [jnp.where(first_half, v, zero), jnp.where(first_half, zero, v)], axis=1
                )
                s = jnp.where(pair_mask, dot(key_t[:, at], v2), 0.0).astype(BF16)
                o = dot(query[at], s)
                heads += [o[:64, :D], o[64:, D:]]
            mixed = normalize(jnp.concatenate(heads, axis=0), hg[2:3]) * sigmoid(tail[:, D:])
            res = dot(mixed.astype(BF16), wout[2])
            for c in range(4):
                col_res[pl.ds(4 * group + c, 64, stride=UNIT), :] = res[64 * c : 64 * c + 64]
        col_out[:, :, u] = col_res[...].astype(BF16).reshape(N_ROW, ROW_DEV, UNIT, D)

    groups = [group for groups in BACK for group in groups]

    def send_back(g, steps):
        (u0, u1), (i0, i1) = groups[g]
        rows, units = pl.ds(i0, i1 - i0), pl.ds(u0, u1 - u0)
        for step in steps:
            peer = row_peer(step)
            pltpu.make_async_remote_copy(
                src_ref=col_out.at[peer, rows, units],
                dst_ref=ret.at[row, rows, units],
                send_sem=r_send,
                recv_sem=r_recv.at[g],
                device_id=(peer, col),
                device_id_type=MESH,
            ).start()

    def column_chunk(k):
        with jax.named_scope("f_wait"):
            arrived(col_in.at[:, :, pl.ds(FORWARD[k][0], FORWARD[k][1] - FORWARD[k][0])], f_recv.at[k])
        for u in range(*FORWARD[k]):
            with jax.named_scope("col_pass"):
                column_pass(u)
            for g, steps in ISSUE[u]:
                send_back(g, steps)
            ret[row, :, u] = col_out[row, :, u]

    column_chunk(0)

    with jax.named_scope("rs_wait"):
        arrived(part_in.at[: N_COL - 1], s_recv)
    total = part_in[...].astype(F32).sum(axis=0)
    slice_of(state, col)[...] = total.astype(BF16)
    for step in COL_STEPS:
        peer = col_peer(step)
        pltpu.make_async_remote_copy(
            src_ref=slice_of(state, col),
            dst_ref=slice_of(state, col),
            send_sem=g_send,
            recv_sem=g_recv,
            device_id=(row, peer),
            device_id_type=MESH,
        ).start()

    for k in range(1, len(FORWARD)):
        column_chunk(k)

    with jax.named_scope("ag_wait"):
        arrived(part_in.at[: N_COL - 1], g_recv)

    def row_close(i, carry):
        acc = x[i].reshape(512, D).astype(F32)
        for p in range(2):
            s = state[p, i]
            s = jnp.concatenate([s, s, s, s], axis=0)
            s = jnp.where(head_mask, s, jnp.zeros_like(s))
            mixed = normalize(dot(q_keep[p, i], s), hg[p : p + 1]) * gate_keep[p, i]
            acc = acc + dot(mixed.astype(BF16), wout[p]).astype(BF16).astype(F32)
        upd[i] = acc.reshape(N_ROW, UNITS, UNIT, D)
        return carry

    with jax.named_scope('row_close'):
        lax.fori_loop(0, ROW_DEV, row_close, 0, unroll=True)

    for g, ((u0, u1), (i0, i1)) in enumerate(groups):
        with jax.named_scope("r_wait"):
            arrived(ret.at[: N_ROW - 1, pl.ds(i0, i1 - i0), pl.ds(u0, u1 - u0)], r_recv.at[g])
        with jax.named_scope("trans"):
            for u in range(u0, u1):
                for i in range(i0, i1, 2):
                    both = [upd[r, :, u] + ret[:, r, u].astype(F32) for r in (i, i + 1)]
                    v = jnp.concatenate(both, axis=0).reshape(2 * N_ROW * UNIT, D)
                    if g == len(groups) - 1:
                        last[...] = v
                    else:
                        res = transition(v, tg, up, down).reshape(2, N_ROW, UNIT, D)
                        out_ref[i, :, u] = res[0]
                        out_ref[i + 1, :, u] = res[1]

    arrived(col_in.at[: N_ROW - 1], f_send)
    arrived(part_in.at[: N_COL - 1], s_send)
    arrived(part_in.at[: N_COL - 1], g_send)
    arrived(col_out.at[: N_ROW - 1], r_send)


def finish(most, last, tg, up, down, out, rest, sem):
    copies = [
        pltpu.make_async_copy(most.at[i, :, :3], out.at[i, :, :3], sem.at[i]) for i in range(ROW_DEV)
    ]
    copies.append(pltpu.make_async_copy(most.at[:2, :, 3], out.at[:2, :, 3], sem.at[4]))
    for copy in copies:
        copy.start()
    rest[...] = transition(last[...], tg, up, down).reshape(2, N_ROW, UNIT, D)
    copies.append(pltpu.make_async_copy(rest, out.at[2:, :, 3], sem.at[5]))
    copies[-1].start()
    for copy in copies:
        copy.wait()


def shards(x, norm_gain, in_weights, head_gain, out_weights, trans_gain, up_weight, down_weight):
    any_spec = pl.BlockSpec(memory_space=pl.ANY)
    dma = pltpu.SemaphoreType.DMA
    parts = pl.pallas_call(
        kernel,
        out_shape=[
            pltpu.VMEM((ROW_DEV, N_ROW, UNITS, UNIT, D), BF16),
            pltpu.VMEM((2 * N_ROW * UNIT, D), F32),
            pltpu.VMEM((1, D), F32),
            pltpu.VMEM((D, FF), BF16),
            pltpu.VMEM((FF, D), BF16),
        ],
        in_specs=[any_spec] * 8,
        out_specs=[pl.BlockSpec(memory_space=pltpu.VMEM)] * 5,
        scratch_shapes=[
            pltpu.VMEM((ROW_DEV, N_ROW, UNITS, UNIT, D), BF16),
            pltpu.VMEM((1, D), F32),
            pltpu.VMEM((3, D, 4 * D), BF16),
            pltpu.VMEM((3, D), F32),
            pltpu.VMEM((3, D, D), BF16),
            pltpu.VMEM((3, D, D), BF16),
            pltpu.VMEM((2, ROW_DEV, 512, D), BF16),
            pltpu.VMEM((2, ROW_DEV, 512, D), F32),
            pltpu.VMEM((ROW_DEV, N_ROW, UNITS, UNIT, D), F32),
            pltpu.VMEM((2, ROW_DEV, HEAD, D), BF16),
            pltpu.VMEM((N_COL, 16, D), BF16),
            pltpu.VMEM((2, ROW_DEV, HEAD, D), BF16),
            pltpu.VMEM((N_ROW, ROW_DEV, UNITS, UNIT, D), BF16),
            pltpu.VMEM((64 * UNIT, D), F32),
            pltpu.VMEM((64 * UNIT, D), F32),
            pltpu.VMEM((N_ROW, ROW_DEV, UNITS, UNIT, D), BF16),
            pltpu.VMEM((N_ROW, ROW_DEV, UNITS, UNIT, D), BF16),
            dma((2,)), dma(()), dma((len(FORWARD),)), dma(()), dma((sum(map(len, BACK)),)),
            dma(()), dma(()), dma(()), dma(()),
            pltpu.SemaphoreType.REGULAR((2,)), pltpu.SemaphoreType.REGULAR((3,)),
        ],
        compiler_params=pltpu.CompilerParams(
            collective_id=0, has_side_effects=True, vmem_limit_bytes=60 * 1024 * 1024
        ),
    )(
        x.reshape(ROW_DEV, N_ROW, UNITS, UNIT, D), norm_gain.reshape(1, D), in_weights, head_gain,
        out_weights, trans_gain.reshape(1, D), up_weight, down_weight,
    )
    out = pl.pallas_call(
        finish,
        out_shape=jax.ShapeDtypeStruct((ROW_DEV, N_ROW, UNITS, UNIT, D), BF16),
        in_specs=[pl.BlockSpec(memory_space=pltpu.VMEM)] * 5,
        out_specs=any_spec,
        scratch_shapes=[pltpu.VMEM((2, N_ROW, UNIT, D), BF16), dma((6,))],
        compiler_params=pltpu.CompilerParams(vmem_limit_bytes=8 * 1024 * 1024),
    )(*(pltpu.with_memory_space_constraint(part, pltpu.VMEM) for part in parts))
    return out.reshape(x.shape)


def solution(mesh):
    in_specs = (P("row", "col", None), P(), P(), P(), P(), P(), P(), P())
    return jax.shard_map(
        shards, mesh=mesh, in_specs=in_specs, out_specs=P("row", "col", None), check_vma=False
    )
```

```python
import jax
import jax.numpy as jnp
from jax import lax
from jax.experimental import pallas as pl
from jax.experimental.pallas import tpu as pltpu
from jax.sharding import PartitionSpec as P

D = 128
HEADS = 4
HEAD = 32
FF = 512
N_ROW = 16
N_COL = 16
ROW_DEV = 4
UNITS = 4
UNIT = 8
FORWARD = [(0, 1), (1, 2), (2, 4)]
BACK = [[((0, 1), (0, 4)), ((1, 2), (0, 4))], [((2, 3), (0, 4)), ((3, 4), (0, 2)), ((3, 4), (2, 4))]]
EPS = 1e-05
MESH = pl.DeviceIdType.MESH
F32 = jnp.float32
BF16 = jnp.bfloat16

ROW_STAGES = [
    [(0, 2), (0, 6), (0, 1), (0, 7), (1, 0)],
    [(0, 4), (0, 3), (0, 5), (1, 2), (1, 6), (1, 1), (1, 7)],
    [(1, 4), (1, 3), (1, 5)],
]
ROW_STEPS = [step for stage in ROW_STAGES[::-1] for step in stage]
FAR, NEAR = ROW_STEPS[:8], ROW_STEPS[8:]
ISSUE = [[(0, ROW_STEPS)], [(1, ROW_STEPS)], [(2, FAR)], [(3, FAR), (4, FAR), (2, NEAR), (3, NEAR), (4, NEAR)]]
COL_STEPS = [
    (dx, dl, dc) for dx in (2, 1, 3, 0) for dl in (1, 0) for dc in (1, 0) if (dx, dl, dc) != (0, 0, 0)
]
FILL = ([(k, step) for k in (1, 2) for step in ROW_STAGES[0][:4]], [])
COL_NEXT = [(1, 0, 0), (3, 0, 0), (0, 1, 0), (0, 0, 1)]


def arrived(ref, sem):
    pltpu.make_async_copy(ref, ref, sem).wait()


def dot(a, b):
    return jnp.dot(a, b, preferred_element_type=F32)


def dot_t(a, b):
    return lax.dot_general(a, b, (((1,), (1,)), ((), ())), preferred_element_type=F32)


def feature(v):
    return jnp.maximum(v, 0.0) + jnp.exp(jnp.minimum(v, 0.0))


def sigmoid(v):
    return 0.5 * jnp.tanh(0.5 * v) + 0.5


def normalize(v, gain):
    meansq = jnp.mean(v * v, axis=-1, keepdims=True)
    return v * lax.rsqrt(meansq + EPS) * gain


def transition(v, tg, up, down):
    hid = dot(normalize(v, tg[...]).astype(BF16), up[...])
    hid = (hid * sigmoid(hid)).astype(BF16)
    return (v + dot(hid, down[...])).astype(BF16)


def same_head(rows, columns):
    r = lax.broadcasted_iota(jnp.int32, (rows, columns), 0) % D // HEAD
    c = lax.broadcasted_iota(jnp.int32, (rows, columns), 1) % D // HEAD
    return r == c


def kernel(
    x_hbm, ng_hbm, win_hbm, hg_hbm, wout_hbm, tg_hbm, up_hbm, down_hbm,
    out_ref, last, tg, up, down,
    x, ng, win, hg, wout,
    wkt, q_keep, gate_keep, upd,
    part, part_in, state, col_in, col_norm, col_res, col_out, ret,
    local_sem, f_send, f_recv, r_send, r_recv, s_send, s_recv, g_send, g_recv, row_in, col_told,
):
    row = lax.axis_index("row")
    col = lax.axis_index("col")
    y_hi, z = row // 8, row % 8
    cx, cl, cc = col // 4, (col // 2) % 2, col % 2

    def row_peer(step):
        return ((y_hi + step[0]) % 2) * 8 + (z + step[1]) % 8

    def col_peer(step):
        return ((cx + step[0]) % 4) * 4 + ((cl + step[1]) % 2) * 2 + (cc + step[2]) % 2

    def tell_row(sem, steps):
        for step in steps:
            pl.semaphore_signal(sem, 1, device_id=(row_peer(step), col), device_id_type=MESH)

    def tell_col(sem):
        for step in COL_NEXT:
            pl.semaphore_signal(sem, 1, device_id=(row, col_peer(step)), device_id_type=MESH)

    barrier = pltpu.get_barrier_semaphore()
    tell_row(barrier, ROW_STAGES[0])
    tell_col(barrier)
    loads = [
        pltpu.make_async_copy(src, dst, local_sem.at[int(k > 0)])
        for k, (src, dst) in enumerate(
            [
                (x_hbm, x), (ng_hbm, ng), (win_hbm, win), (hg_hbm, hg),
                (wout_hbm, wout), (tg_hbm, tg), (up_hbm, up), (down_hbm, down),
            ]
        )
    ]
    for load in loads:
        load.start()
    for k, (u0, u1) in enumerate(FORWARD):
        units = pl.ds(u0, u1 - u0)
        pltpu.make_async_copy(
            x_hbm.at[:, row, units], col_in.at[row, :, units], f_recv.at[k]
        ).start()

    def send_forward(k, step):
        peer = row_peer(step)
        units = pl.ds(FORWARD[k][0], FORWARD[k][1] - FORWARD[k][0])
        pltpu.make_async_remote_copy(
            src_ref=x_hbm.at[:, peer, units],
            dst_ref=col_in.at[row, :, units],
            send_sem=f_send,
            recv_sem=f_recv.at[k],
            device_id=(peer, col),
            device_id_type=MESH,
        ).start()

    with jax.named_scope("bar"):
        pl.semaphore_wait(barrier, len(ROW_STAGES[0]) + len(COL_NEXT))
    near = ROW_STAGES[0][:4]
    tell_row(row_in.at[0], near)
    tell_col(col_told.at[0])
    for step in ROW_STAGES[0]:
        send_forward(0, step)
    for k, step in FILL[0]:
        send_forward(k, step)
    with jax.named_scope("stage"):
        pl.semaphore_wait(row_in.at[0], len(near))
    tell_row(row_in.at[1], [(1, 0)])
    for step in ROW_STAGES[1]:
        send_forward(0, step)
    for k, step in FILL[1]:
        send_forward(k, step)
    pl.semaphore_wait(col_told.at[0], len(COL_NEXT))
    tell_col(col_told.at[1])
    with jax.named_scope("stage"):
        pl.semaphore_wait(row_in.at[1], 1)
    for step in ROW_STAGES[2]:
        send_forward(0, step)
    for k in range(1, len(FORWARD)):
        for step in ROW_STEPS:
            if (k, step) not in FILL[0] + FILL[1]:
                send_forward(k, step)
    pl.semaphore_wait(col_told.at[1], len(COL_NEXT))
    tell_col(col_told.at[2])

    with jax.named_scope("loads"):
      for load in loads:
        load.wait()
    for p in range(3):
        wkt[p] = win[p, :, D : 2 * D].astype(F32).T.astype(BF16)

    head_mask = same_head(D, D)

    def row_open(i, carry):
        normed = normalize(x[i].reshape(512, D).astype(F32), ng[...]).astype(BF16)
        for p in range(2):
            q_keep[p, i] = feature(dot(normed, win[p, :, :D])).astype(BF16)
            key_t = feature(dot_t(wkt[p], normed)).astype(BF16)
            tail = dot(normed, win[p, :, 2 * D :])
            gate_keep[p, i] = sigmoid(tail[:, D:])
            full = dot(key_t, tail[:, :D].astype(BF16))
            full = jnp.where(head_mask, full, 0.0).reshape(HEADS, HEAD, D).sum(axis=0)
            part[p, i] = full.astype(BF16)
        return carry

    with jax.named_scope('row_open'):
        lax.fori_loop(0, ROW_DEV, row_open, 0, unroll=True)
    pl.semaphore_wait(col_told.at[2], len(COL_NEXT))

    def slice_of(ref, at):
        return ref.at[at // 8, (at // 2) % 4, pl.ds((at % 2) * 16, 16)]

    for step in COL_STEPS:
        peer = col_peer(step)
        pltpu.make_async_remote_copy(
            src_ref=slice_of(part, peer),
            dst_ref=part_in.at[col],
            send_sem=s_send,
            recv_sem=s_recv,
            device_id=(row, peer),
            device_id_type=MESH,
        ).start()
    part_in[col] = slice_of(part, col)[...]

    first_half = lax.broadcasted_iota(jnp.int32, (D, D), 0) < 64
    pair_mask = same_head(D, 2 * D)

    def column_pass(u):
        block = col_in[:, :, u].reshape(64 * UNIT, D).astype(F32)
        col_norm[...] = normalize(block, ng[...])
        for group in range(UNIT // 4):
            normed = jnp.concatenate(
                [col_norm[pl.ds(4 * group + c, 64, stride=UNIT), :] for c in range(4)], axis=0
            ).astype(BF16)
            query = feature(dot(normed, win[2, :, :D])).astype(BF16)
            key_t = feature(dot_t(wkt[2], normed)).astype(BF16)
            tail = dot(normed, win[2, :, 2 * D :])
            value = tail[:, :D].astype(BF16)
            heads = []
            for pair in range(2):
                at = slice(D * pair, D * pair + D)
                v = value[at]
                zero = jnp.zeros_like(v)
                v2 = jnp.concatenate(
                    [jnp.where(first_half, v, zero), jnp.where(first_half, zero, v)], axis=1
                )
                s = jnp.where(pair_mask, dot(key_t[:, at], v2), 0.0).astype(BF16)
                o = dot(query[at], s)
                heads += [o[:64, :D], o[64:, D:]]
            mixed = normalize(jnp.concatenate(heads, axis=0), hg[2:3]) * sigmoid(tail[:, D:])
            res = dot(mixed.astype(BF16), wout[2])
            for c in range(4):
                col_res[pl.ds(4 * group + c, 64, stride=UNIT), :] = res[64 * c : 64 * c + 64]
        col_out[:, :, u] = col_res[...].astype(BF16).reshape(N_ROW, ROW_DEV, UNIT, D)

    groups = [group for groups in BACK for group in groups]

    def send_back(g, steps):
        (u0, u1), (i0, i1) = groups[g]
        rows, units = pl.ds(i0, i1 - i0), pl.ds(u0, u1 - u0)
        for step in steps:
            peer = row_peer(step)
            pltpu.make_async_remote_copy(
                src_ref=col_out.at[peer, rows, units],
                dst_ref=ret.at[row, rows, units],
                send_sem=r_send,
                recv_sem=r_recv.at[g],
                device_id=(peer, col),
                device_id_type=MESH,
            ).start()

    def column_chunk(k):
        with jax.named_scope("f_wait"):
            arrived(col_in.at[:, :, pl.ds(FORWARD[k][0], FORWARD[k][1] - FORWARD[k][0])], f_recv.at[k])
        for u in range(*FORWARD[k]):
            with jax.named_scope("col_pass"):
                column_pass(u)
            ret[row, :, u] = col_out[row, :, u]
            for g, steps in ISSUE[u]:
                send_back(g, steps)

    column_chunk(0)

    with jax.named_scope("rs_wait"):
        arrived(part_in.at[: N_COL - 1], s_recv)
    total = part_in[...].astype(F32).sum(axis=0)
    slice_of(state, col)[...] = total.astype(BF16)
    for step in COL_STEPS:
        peer = col_peer(step)
        pltpu.make_async_remote_copy(
            src_ref=slice_of(state, col),
            dst_ref=slice_of(state, col),
            send_sem=g_send,
            recv_sem=g_recv,
            device_id=(row, peer),
            device_id_type=MESH,
        ).start()

    for k in range(1, len(FORWARD)):
        column_chunk(k)

    with jax.named_scope("ag_wait"):
        arrived(part_in.at[: N_COL - 1], g_recv)

    def row_close(i, carry):
        acc = x[i].reshape(512, D).astype(F32)
        for p in range(2):
            s = state[p, i]
            s = jnp.concatenate([s, s, s, s], axis=0)
            s = jnp.where(head_mask, s, jnp.zeros_like(s))
            mixed = normalize(dot(q_keep[p, i], s), hg[p : p + 1]) * gate_keep[p, i]
            acc = acc + dot(mixed.astype(BF16), wout[p]).astype(BF16).astype(F32)
        upd[i] = acc.reshape(N_ROW, UNITS, UNIT, D)
        return carry

    with jax.named_scope('row_close'):
        lax.fori_loop(0, ROW_DEV, row_close, 0, unroll=True)

    for g, ((u0, u1), (i0, i1)) in enumerate(groups):
        with jax.named_scope("r_wait"):
            arrived(ret.at[: N_ROW - 1, pl.ds(i0, i1 - i0), pl.ds(u0, u1 - u0)], r_recv.at[g])
        with jax.named_scope("trans"):
            for u in range(u0, u1):
                for i in range(i0, i1, 2):
                    both = [upd[r, :, u] + ret[:, r, u].astype(F32) for r in (i, i + 1)]
                    v = jnp.concatenate(both, axis=0).reshape(2 * N_ROW * UNIT, D)
                    if g == len(groups) - 1:
                        last[...] = v
                    else:
                        res = transition(v, tg, up, down).reshape(2, N_ROW, UNIT, D)
                        out_ref[i, :, u] = res[0]
                        out_ref[i + 1, :, u] = res[1]

    arrived(col_in.at[: N_ROW - 1], f_send)
    arrived(part_in.at[: N_COL - 1], s_send)
    arrived(part_in.at[: N_COL - 1], g_send)
    arrived(col_out.at[: N_ROW - 1], r_send)


def finish(most, last, tg, up, down, out, rest, sem):
    copies = [
        pltpu.make_async_copy(most.at[i, :, :3], out.at[i, :, :3], sem.at[i]) for i in range(ROW_DEV)
    ]
    copies.append(pltpu.make_async_copy(most.at[:2, :, 3], out.at[:2, :, 3], sem.at[4]))
    for copy in copies:
        copy.start()
    rest[...] = transition(last[...], tg, up, down).reshape(2, N_ROW, UNIT, D)
    copies.append(pltpu.make_async_copy(rest, out.at[2:, :, 3], sem.at[5]))
    copies[-1].start()
    for copy in copies:
        copy.wait()


def shards(x, norm_gain, in_weights, head_gain, out_weights, trans_gain, up_weight, down_weight):
    any_spec = pl.BlockSpec(memory_space=pl.ANY)
    dma = pltpu.SemaphoreType.DMA
    parts = pl.pallas_call(
        kernel,
        out_shape=[
            pltpu.VMEM((ROW_DEV, N_ROW, UNITS, UNIT, D), BF16),
            pltpu.VMEM((2 * N_ROW * UNIT, D), F32),
            pltpu.VMEM((1, D), F32),
            pltpu.VMEM((D, FF), BF16),
            pltpu.VMEM((FF, D), BF16),
        ],
        in_specs=[any_spec] * 8,
        out_specs=[pl.BlockSpec(memory_space=pltpu.VMEM)] * 5,
        scratch_shapes=[
            pltpu.VMEM((ROW_DEV, N_ROW, UNITS, UNIT, D), BF16),
            pltpu.VMEM((1, D), F32),
            pltpu.VMEM((3, D, 4 * D), BF16),
            pltpu.VMEM((3, D), F32),
            pltpu.VMEM((3, D, D), BF16),
            pltpu.VMEM((3, D, D), BF16),
            pltpu.VMEM((2, ROW_DEV, 512, D), BF16),
            pltpu.VMEM((2, ROW_DEV, 512, D), F32),
            pltpu.VMEM((ROW_DEV, N_ROW, UNITS, UNIT, D), F32),
            pltpu.VMEM((2, ROW_DEV, HEAD, D), BF16),
            pltpu.VMEM((N_COL, 16, D), BF16),
            pltpu.VMEM((2, ROW_DEV, HEAD, D), BF16),
            pltpu.VMEM((N_ROW, ROW_DEV, UNITS, UNIT, D), BF16),
            pltpu.VMEM((64 * UNIT, D), F32),
            pltpu.VMEM((64 * UNIT, D), F32),
            pltpu.VMEM((N_ROW, ROW_DEV, UNITS, UNIT, D), BF16),
            pltpu.VMEM((N_ROW, ROW_DEV, UNITS, UNIT, D), BF16),
            dma((2,)), dma(()), dma((len(FORWARD),)), dma(()), dma((sum(map(len, BACK)),)),
            dma(()), dma(()), dma(()), dma(()),
            pltpu.SemaphoreType.REGULAR((2,)), pltpu.SemaphoreType.REGULAR((3,)),
        ],
        compiler_params=pltpu.CompilerParams(
            collective_id=0, has_side_effects=True, vmem_limit_bytes=60 * 1024 * 1024
        ),
    )(
        x.reshape(ROW_DEV, N_ROW, UNITS, UNIT, D), norm_gain.reshape(1, D), in_weights, head_gain,
        out_weights, trans_gain.reshape(1, D), up_weight, down_weight,
    )
    out = pl.pallas_call(
        finish,
        out_shape=jax.ShapeDtypeStruct((ROW_DEV, N_ROW, UNITS, UNIT, D), BF16),
        in_specs=[pl.BlockSpec(memory_space=pltpu.VMEM)] * 5,
        out_specs=any_spec,
        scratch_shapes=[pltpu.VMEM((2, N_ROW, UNIT, D), BF16), dma((6,))],
        compiler_params=pltpu.CompilerParams(vmem_limit_bytes=8 * 1024 * 1024),
    )(*(pltpu.with_memory_space_constraint(part, pltpu.VMEM) for part in parts))
    return out.reshape(x.shape)


def solution(mesh):
    in_specs = (P("row", "col", None), P(), P(), P(), P(), P(), P(), P())
    return jax.shard_map(
        shards, mesh=mesh, in_specs=in_specs, out_specs=P("row", "col", None), check_vma=False
    )
```

```python
import jax
import jax.numpy as jnp
from jax import lax
from jax.experimental import pallas as pl
from jax.experimental.pallas import tpu as pltpu
from jax.sharding import PartitionSpec as P

D = 128
HEADS = 4
HEAD = 32
FF = 512
N_ROW = 16
N_COL = 16
ROW_DEV = 4
UNITS = 4
UNIT = 8
FORWARD = [(0, 1), (1, 2), (2, 4)]
BACK = [[((0, 1), (0, 4)), ((1, 2), (0, 4))], [((2, 3), (0, 4)), ((3, 4), (0, 2)), ((3, 4), (2, 4))]]
EPS = 1e-05
MESH = pl.DeviceIdType.MESH
F32 = jnp.float32
BF16 = jnp.bfloat16

ROW_STAGES = [
    [(0, 2), (0, 6), (0, 1), (0, 7), (1, 0)],
    [(0, 4), (0, 3), (0, 5), (1, 2), (1, 6), (1, 1), (1, 7)],
    [(1, 4), (1, 3), (1, 5)],
]
ROW_STEPS = [step for stage in ROW_STAGES[::-1] for step in stage]
FAR, NEAR = ROW_STEPS[:8], ROW_STEPS[8:]
ISSUE = [[(0, ROW_STEPS)], [(1, ROW_STEPS)], [(2, FAR)], [(3, FAR), (4, FAR), (2, NEAR), (3, NEAR), (4, NEAR)]]
COL_STEPS = [
    (dx, dl, dc) for dx in (2, 1, 3, 0) for dl in (1, 0) for dc in (1, 0) if (dx, dl, dc) != (0, 0, 0)
]
FILL = ([(k, step) for k in (1, 2) for step in ROW_STAGES[0][:4]], [])
COL_NEXT = [(1, 0, 0), (3, 0, 0), (0, 1, 0), (0, 0, 1)]


def arrived(ref, sem):
    pltpu.make_async_copy(ref, ref, sem).wait()


def dot(a, b):
    return jnp.dot(a, b, preferred_element_type=F32)


def dot_t(a, b):
    return lax.dot_general(a, b, (((1,), (1,)), ((), ())), preferred_element_type=F32)


def feature(v):
    return jnp.maximum(v, 0.0) + jnp.exp(jnp.minimum(v, 0.0))


def sigmoid(v):
    return 0.5 * jnp.tanh(0.5 * v) + 0.5


def normalize(v, gain):
    meansq = jnp.mean(v * v, axis=-1, keepdims=True)
    return v * lax.rsqrt(meansq + EPS) * gain


def transition(v, tg, up, down):
    hid = dot(normalize(v, tg[...]).astype(BF16), up[...])
    hid = (hid * sigmoid(hid)).astype(BF16)
    return (v + dot(hid, down[...])).astype(BF16)


def same_head(rows, columns):
    r = lax.broadcasted_iota(jnp.int32, (rows, columns), 0) % D // HEAD
    c = lax.broadcasted_iota(jnp.int32, (rows, columns), 1) % D // HEAD
    return r == c


def kernel(
    x_hbm, ng_hbm, win_hbm, hg_hbm, wout_hbm, tg_hbm, up_hbm, down_hbm,
    out_ref, last, tg, up, down,
    x, ng, win, hg, wout,
    wkt, q_keep, gate_keep, upd,
    part, part_in, state, col_in, col_norm, col_res, col_out, ret,
    local_sem, f_send, f_recv, r_send, r_recv, s_send, s_recv, g_send, g_recv, row_in, col_told,
):
    row = lax.axis_index("row")
    col = lax.axis_index("col")
    y_hi, z = row // 8, row % 8
    cx, cl, cc = col // 4, (col // 2) % 2, col % 2

    def row_peer(step):
        return ((y_hi + step[0]) % 2) * 8 + (z + step[1]) % 8

    def col_peer(step):
        return ((cx + step[0]) % 4) * 4 + ((cl + step[1]) % 2) * 2 + (cc + step[2]) % 2

    def tell_row(sem, steps):
        for step in steps:
            pl.semaphore_signal(sem, 1, device_id=(row_peer(step), col), device_id_type=MESH)

    def tell_col(sem):
        for step in COL_NEXT:
            pl.semaphore_signal(sem, 1, device_id=(row, col_peer(step)), device_id_type=MESH)

    barrier = pltpu.get_barrier_semaphore()
    tell_row(barrier, ROW_STAGES[0])
    tell_col(barrier)
    loads = [
        pltpu.make_async_copy(src, dst, local_sem.at[int(k > 0)])
        for k, (src, dst) in enumerate(
            [
                (x_hbm, x), (ng_hbm, ng), (win_hbm, win), (hg_hbm, hg),
                (wout_hbm, wout), (tg_hbm, tg), (up_hbm, up), (down_hbm, down),
            ]
        )
    ]
    for load in loads:
        load.start()
    for k, (u0, u1) in enumerate(FORWARD):
        units = pl.ds(u0, u1 - u0)
        pltpu.make_async_copy(
            x_hbm.at[:, row, units], col_in.at[row, :, units], f_recv.at[k]
        ).start()

    def send_forward(k, step):
        peer = row_peer(step)
        units = pl.ds(FORWARD[k][0], FORWARD[k][1] - FORWARD[k][0])
        pltpu.make_async_remote_copy(
            src_ref=x_hbm.at[:, peer, units],
            dst_ref=col_in.at[row, :, units],
            send_sem=f_send,
            recv_sem=f_recv.at[k],
            device_id=(peer, col),
            device_id_type=MESH,
        ).start()

    with jax.named_scope("bar"):
        pl.semaphore_wait(barrier, len(ROW_STAGES[0]) + len(COL_NEXT))
    near = ROW_STAGES[0][:4]
    tell_row(row_in.at[0], near)
    tell_col(col_told.at[0])
    for step in ROW_STAGES[0]:
        send_forward(0, step)
    for k, step in FILL[0]:
        send_forward(k, step)
    with jax.named_scope("stage"):
        pl.semaphore_wait(row_in.at[0], len(near))
    tell_row(row_in.at[1], [(1, 0)])
    for step in ROW_STAGES[1]:
        send_forward(0, step)
    for k, step in FILL[1]:
        send_forward(k, step)
    pl.semaphore_wait(col_told.at[0], len(COL_NEXT))
    tell_col(col_told.at[1])
    with jax.named_scope("stage"):
        pl.semaphore_wait(row_in.at[1], 1)
    for step in ROW_STAGES[2]:
        send_forward(0, step)
    for k in range(1, len(FORWARD)):
        for step in ROW_STEPS:
            if (k, step) not in FILL[0] + FILL[1]:
                send_forward(k, step)
    pl.semaphore_wait(col_told.at[1], len(COL_NEXT))
    tell_col(col_told.at[2])

    with jax.named_scope("loads"):
      for load in loads:
        load.wait()
    for p in range(3):
        wkt[p] = win[p, :, D : 2 * D].astype(F32).T.astype(BF16)

    head_mask = same_head(D, D)

    def row_open(i, carry):
        normed = normalize(x[i].reshape(512, D).astype(F32), ng[...]).astype(BF16)
        for p in range(2):
            q_keep[p, i] = feature(dot(normed, win[p, :, :D])).astype(BF16)
            key_t = feature(dot_t(wkt[p], normed)).astype(BF16)
            tail = dot(normed, win[p, :, 2 * D :])
            gate_keep[p, i] = sigmoid(tail[:, D:])
            full = dot(key_t, tail[:, :D].astype(BF16))
            full = jnp.where(head_mask, full, 0.0).reshape(HEADS, HEAD, D).sum(axis=0)
            part[p, i] = full.astype(BF16)
        return carry

    with jax.named_scope('row_open'):
        lax.fori_loop(0, ROW_DEV, row_open, 0, unroll=True)
    pl.semaphore_wait(col_told.at[2], len(COL_NEXT))

    def slice_of(ref, at):
        return ref.at[at // 8, (at // 2) % 4, pl.ds((at % 2) * 16, 16)]

    for step in COL_STEPS:
        peer = col_peer(step)
        pltpu.make_async_remote_copy(
            src_ref=slice_of(part, peer),
            dst_ref=part_in.at[col],
            send_sem=s_send,
            recv_sem=s_recv,
            device_id=(row, peer),
            device_id_type=MESH,
        ).start()
    part_in[col] = slice_of(part, col)[...]

    first_half = lax.broadcasted_iota(jnp.int32, (D, D), 0) < 64
    pair_mask = same_head(D, 2 * D)

    def column_pass(u):
        block = col_in[:, :, u].reshape(64 * UNIT, D).astype(F32)
        col_norm[...] = normalize(block, ng[...])
        for group in range(UNIT // 4):
            normed = jnp.concatenate(
                [col_norm[pl.ds(4 * group + c, 64, stride=UNIT), :] for c in range(4)], axis=0
            ).astype(BF16)
            query = feature(dot(normed, win[2, :, :D])).astype(BF16)
            key_t = feature(dot_t(wkt[2], normed)).astype(BF16)
            tail = dot(normed, win[2, :, 2 * D :])
            value = tail[:, :D].astype(BF16)
            heads = []
            for pair in range(2):
                at = slice(D * pair, D * pair + D)
                v = value[at]
                zero = jnp.zeros_like(v)
                v2 = jnp.concatenate(
                    [jnp.where(first_half, v, zero), jnp.where(first_half, zero, v)], axis=1
                )
                s = jnp.where(pair_mask, dot(key_t[:, at], v2), 0.0).astype(BF16)
                o = dot(query[at], s)
                heads += [o[:64, :D], o[64:, D:]]
            mixed = normalize(jnp.concatenate(heads, axis=0), hg[2:3]) * sigmoid(tail[:, D:])
            res = dot(mixed.astype(BF16), wout[2])
            for c in range(4):
                col_res[pl.ds(4 * group + c, 64, stride=UNIT), :] = res[64 * c : 64 * c + 64]
        col_out[:, :, u] = col_res[...].astype(BF16).reshape(N_ROW, ROW_DEV, UNIT, D)

    groups = [group for groups in BACK for group in groups]

    def send_back(g, steps):
        (u0, u1), (i0, i1) = groups[g]
        rows, units = pl.ds(i0, i1 - i0), pl.ds(u0, u1 - u0)
        for step in steps:
            peer = row_peer(step)
            pltpu.make_async_remote_copy(
                src_ref=col_out.at[peer, rows, units],
                dst_ref=ret.at[row, rows, units],
                send_sem=r_send,
                recv_sem=r_recv.at[g],
                device_id=(peer, col),
                device_id_type=MESH,
            ).start()

    def column_chunk(k):
        with jax.named_scope("f_wait"):
            arrived(col_in.at[:, :, pl.ds(FORWARD[k][0], FORWARD[k][1] - FORWARD[k][0])], f_recv.at[k])
        for u in range(*FORWARD[k]):
            with jax.named_scope("col_pass"):
                column_pass(u)
            ret[row, :, u] = col_out[row, :, u]
            for g, steps in ISSUE[u]:
                send_back(g, steps)

    column_chunk(0)

    with jax.named_scope("rs_wait"):
        arrived(part_in.at[: N_COL - 1], s_recv)
    total = part_in[...].astype(F32).sum(axis=0)
    slice_of(state, col)[...] = total.astype(BF16)
    for step in COL_STEPS:
        peer = col_peer(step)
        pltpu.make_async_remote_copy(
            src_ref=slice_of(state, col),
            dst_ref=slice_of(state, col),
            send_sem=g_send,
            recv_sem=g_recv,
            device_id=(row, peer),
            device_id_type=MESH,
        ).start()

    for k in range(1, len(FORWARD)):
        column_chunk(k)

    with jax.named_scope("ag_wait"):
        arrived(part_in.at[: N_COL - 1], g_recv)

    def row_close(i, carry):
        acc = x[i].reshape(512, D).astype(F32)
        for p in range(2):
            s = state[p, i]
            s = jnp.concatenate([s, s, s, s], axis=0)
            s = jnp.where(head_mask, s, jnp.zeros_like(s))
            mixed = normalize(dot(q_keep[p, i], s), hg[p : p + 1]) * gate_keep[p, i]
            acc = acc + dot(mixed.astype(BF16), wout[p]).astype(BF16).astype(F32)
        upd[i] = acc.reshape(N_ROW, UNITS, UNIT, D)
        return carry

    with jax.named_scope('row_close'):
        lax.fori_loop(0, ROW_DEV, row_close, 0, unroll=True)

    for g, ((u0, u1), (i0, i1)) in enumerate(groups):
        with jax.named_scope("r_wait"):
            arrived(ret.at[: N_ROW - 1, pl.ds(i0, i1 - i0), pl.ds(u0, u1 - u0)], r_recv.at[g])
        with jax.named_scope("trans"):
            for u in range(u0, u1):
                for i in range(i0, i1, 2):
                    both = [upd[r, :, u] + ret[:, r, u].astype(F32) for r in (i, i + 1)]
                    v = jnp.concatenate(both, axis=0).reshape(2 * N_ROW * UNIT, D)
                    if u == UNITS - 1:
                        last[i * N_ROW * UNIT : (i + 2) * N_ROW * UNIT] = v
                    else:
                        res = transition(v, tg, up, down).reshape(2, N_ROW, UNIT, D)
                        out_ref[i, :, u] = res[0]
                        out_ref[i + 1, :, u] = res[1]

    arrived(col_in.at[: N_ROW - 1], f_send)
    arrived(part_in.at[: N_COL - 1], s_send)
    arrived(part_in.at[: N_COL - 1], g_send)
    arrived(col_out.at[: N_ROW - 1], r_send)


def finish(most, last, tg, up, down, out, rest, sem):
    copies = [
        pltpu.make_async_copy(most.at[i, :, :3], out.at[i, :, :3], sem.at[i]) for i in range(ROW_DEV)
    ]
    for copy in copies:
        copy.start()
    rest[...] = transition(last[...], tg, up, down).reshape(ROW_DEV, N_ROW, UNIT, D)
    copies.append(pltpu.make_async_copy(rest, out.at[:, :, 3], sem.at[4]))
    copies[-1].start()
    for copy in copies:
        copy.wait()


def shards(x, norm_gain, in_weights, head_gain, out_weights, trans_gain, up_weight, down_weight):
    any_spec = pl.BlockSpec(memory_space=pl.ANY)
    dma = pltpu.SemaphoreType.DMA
    parts = pl.pallas_call(
        kernel,
        out_shape=[
            pltpu.VMEM((ROW_DEV, N_ROW, UNITS, UNIT, D), BF16),
            pltpu.VMEM((ROW_DEV * N_ROW * UNIT, D), F32),
            pltpu.VMEM((1, D), F32),
            pltpu.VMEM((D, FF), BF16),
            pltpu.VMEM((FF, D), BF16),
        ],
        in_specs=[any_spec] * 8,
        out_specs=[pl.BlockSpec(memory_space=pltpu.VMEM)] * 5,
        scratch_shapes=[
            pltpu.VMEM((ROW_DEV, N_ROW, UNITS, UNIT, D), BF16),
            pltpu.VMEM((1, D), F32),
            pltpu.VMEM((3, D, 4 * D), BF16),
            pltpu.VMEM((3, D), F32),
            pltpu.VMEM((3, D, D), BF16),
            pltpu.VMEM((3, D, D), BF16),
            pltpu.VMEM((2, ROW_DEV, 512, D), BF16),
            pltpu.VMEM((2, ROW_DEV, 512, D), F32),
            pltpu.VMEM((ROW_DEV, N_ROW, UNITS, UNIT, D), F32),
            pltpu.VMEM((2, ROW_DEV, HEAD, D), BF16),
            pltpu.VMEM((N_COL, 16, D), BF16),
            pltpu.VMEM((2, ROW_DEV, HEAD, D), BF16),
            pltpu.VMEM((N_ROW, ROW_DEV, UNITS, UNIT, D), BF16),
            pltpu.VMEM((64 * UNIT, D), F32),
            pltpu.VMEM((64 * UNIT, D), F32),
            pltpu.VMEM((N_ROW, ROW_DEV, UNITS, UNIT, D), BF16),
            pltpu.VMEM((N_ROW, ROW_DEV, UNITS, UNIT, D), BF16),
            dma((2,)), dma(()), dma((len(FORWARD),)), dma(()), dma((sum(map(len, BACK)),)),
            dma(()), dma(()), dma(()), dma(()),
            pltpu.SemaphoreType.REGULAR((2,)), pltpu.SemaphoreType.REGULAR((3,)),
        ],
        compiler_params=pltpu.CompilerParams(
            collective_id=0, has_side_effects=True, vmem_limit_bytes=60 * 1024 * 1024
        ),
    )(
        x.reshape(ROW_DEV, N_ROW, UNITS, UNIT, D), norm_gain.reshape(1, D), in_weights, head_gain,
        out_weights, trans_gain.reshape(1, D), up_weight, down_weight,
    )
    out = pl.pallas_call(
        finish,
        out_shape=jax.ShapeDtypeStruct((ROW_DEV, N_ROW, UNITS, UNIT, D), BF16),
        in_specs=[pl.BlockSpec(memory_space=pltpu.VMEM)] * 5,
        out_specs=any_spec,
        scratch_shapes=[pltpu.VMEM((ROW_DEV, N_ROW, UNIT, D), BF16), dma((5,))],
        compiler_params=pltpu.CompilerParams(vmem_limit_bytes=8 * 1024 * 1024),
    )(*(pltpu.with_memory_space_constraint(part, pltpu.VMEM) for part in parts))
    return out.reshape(x.shape)


def solution(mesh):
    in_specs = (P("row", "col", None), P(), P(), P(), P(), P(), P(), P())
    return jax.shard_map(
        shards, mesh=mesh, in_specs=in_specs, out_specs=P("row", "col", None), check_vma=False
    )
```
